256 devices in a mesh: patch: 4 (over x), line: 16 (over z, core), layer: 4 (over y).
Axes of the slice: x: 4, y: 4, z: 8, core: 2. Of those that a mesh axis runs over, the one named last changes fastest.
Arguments:
- elastic: float32 [4, 5, 1024, 2048], P('patch', None, 'line', 'layer'), may hold values from -6 to 6
- acoustic: float32 [4, 3, 1024, 2048], P('patch', None, 'line', 'layer'), may hold values from -6 to 6
- el_media: float32 [4, 3, 1024, 2048], P('patch', None, 'line', 'layer'), may hold values from 0.2 to 1.5
- ac_media: float32 [4, 2, 1024, 2048], P('patch', None, 'line', 'layer'), may hold values from 0.2 to 1.5
- cont_matrix: float32 [128, 20], replicated, may hold values from -1.25 to 1.25
- fringe_cells: int32 [4, 16, 4, 4, 256], P('patch', 'line', 'layer'), may hold values from 0 to 32767, as said below
- donor_cells: int32 [4, 16, 4, 4, 4, 256], P('patch', 'line', 'layer'), may hold values from 0 to 32767
- donor_weights: float32 [4, 16, 4, 4, 4, 256], P('patch', 'line', 'layer'), may hold values from 0 to 1, as said below
- donor_counts: int32 [4, 16, 4, 4], P('patch', 'line', 'layer'), may hold values from 0 to 256, as said below
- el_pair: int32 [4, 1024], P('patch', 'line'), may hold values from 0 to 63
- ac_pair: int32 [4, 1024], P('patch', 'line'), may hold values from 0 to 63
Outputs:
- new_elastic: float32 [4, 5, 1024, 2048], P('patch', None, 'line', 'layer')
- new_acoustic: float32 [4, 3, 1024, 2048], P('patch', None, 'line', 'layer')
The draws below stay inside these ranges and needn't reach their ends.
Inputs may be any that keep to these rules, and one draw needn't show every extreme that they name: `fringe_cells`: within one device the 1024 fringe cells are distinct. `donor_weights`: Positive; the four weights of a slot sum to 1. `donor_counts`: 0 where donor and receiver are the same patch; on every device one donor patch fills all 256 slots.
All inputs are finite; a program needn't handle non-finite values.
Results may differ from the reference program's by a relative error of at most 0.0001.
Values sent between devices are 32-bit elements; how exact they have to be, the bound alone decides.
A program may use at most 128 MiB of HBM per device.

```python
import math
import jax
import jax.numpy as jnp
from jax import lax

NX = 1024
CONT = 128
MATCH = 10
ZD = 512
RCAP = 256
NP = 4
SLABS = 16
LAYERS = 4
XD = 64
NZ = 2048
P_SIZE = 1152
K = 576


def draw_fringe_cells(key, part):
    subkey = jax.random.fold_in(key, 11)
    stride = XD * ZD // (NP * RCAP)
    slots = lax.iota(jnp.int32, NP * RCAP).reshape(NP, RCAP)
    offsets = jax.random.randint(subkey, (NP, SLABS, LAYERS, NP, RCAP), 0, stride)
    return (slots[None, None, None] * stride + offsets).astype(jnp.int32)


def draw_donor_cells(key, part):
    subkey = jax.random.fold_in(key, 12)
    return jax.random.randint(subkey, (NP, SLABS, LAYERS, NP, 4, RCAP), 0, XD * ZD).astype(jnp.int32)


def draw_donor_weights(key, part):
    subkey = jax.random.fold_in(key, 13)
    raw = jax.random.uniform(subkey, (NP, SLABS, LAYERS, NP, 4, RCAP), jnp.float32, 0.1, 1.0)
    total = raw[:, :, :, :, 0] + raw[:, :, :, :, 1] + raw[:, :, :, :, 2] + raw[:, :, :, :, 3]
    return (raw / total[:, :, :, :, None]).astype(jnp.float32)


def draw_donor_counts(key, part):
    subkey = jax.random.fold_in(key, 14)
    first_key, second_key = jax.random.split(subkey)
    offset = jax.random.randint(first_key, (NP, SLABS, LAYERS, 1), 1, NP)
    receiver = lax.iota(jnp.int32, NP).reshape(NP, 1, 1, 1)
    donor = lax.iota(jnp.int32, NP).reshape(1, 1, 1, NP)
    busiest = (receiver + offset) % NP
    light = jax.random.randint(second_key, (NP, SLABS, LAYERS, NP), 1, RCAP // 2 + 1)
    counts = jnp.where(donor == busiest, RCAP, light)
    return jnp.where(donor == receiver, 0, counts).astype(jnp.int32)


def pairing(key, salt):
    subkey = jax.random.fold_in(key, salt)
    local = lax.iota(jnp.int32, NX) % XD
    jitter = jax.random.randint(subkey, (NP, NX), -3, 4)
    return jnp.clip(local[None, :] + jitter, 0, XD - 1).astype(jnp.int32)


def draw_el_pair(key, part):
    return pairing(key, 15)


def draw_ac_pair(key, part):
    return pairing(key, 16)


def block_scale(key, extent, pieces, smallest, top_value):
    level = 1.0
    for dim, parts in pieces:
        draws = jax.random.uniform(jax.random.fold_in(jax.random.fold_in(key, 6), dim), (parts,), jnp.float32, smallest / len(pieces), top_value / len(pieces))
        level = level * jnp.repeat(jnp.exp(draws), extent[dim] // parts).reshape((-1,) + (1,) * (len(extent) - 1 - dim))
    return level


def normal_values(rng, extent, deviation, most, cuts=(), kind=jnp.bfloat16):
    drawn = deviation * jax.random.normal(rng, extent, jnp.float32)
    if cuts:
        drawn = drawn * block_scale(rng, extent, cuts, -0.22, 0.18)
    return jnp.clip(drawn, -most, most).astype(kind)


def setup_inputs(seed: int = 0) -> dict:
    key_of = jax.random.split(jax.random.key(seed), 12)
    elastic = normal_values(key_of[0], (NP, 5, NX, NZ), 1.0, 6.0, ((0, 4), (2, 16), (3, 4)), jnp.float32)
    acoustic = normal_values(key_of[1], (NP, 3, NX, NZ), 1.0, 6.0, ((0, 4), (2, 16), (3, 4)), jnp.float32)
    el_media = jnp.clip(jnp.exp(math.log(1.5) - 2.014903 * jax.random.uniform(key_of[2], (NP, 3, NX, NZ), jnp.float32) ** block_scale(key_of[2], (NP, 3, NX, NZ), ((0, 4), (2, 16), (3, 4)), -0.2, 0.2)), 0.2, 1.5)
    ac_media = jnp.clip(jnp.exp(math.log(1.5) - 2.014903 * jax.random.uniform(key_of[3], (NP, 2, NX, NZ), jnp.float32) ** block_scale(key_of[3], (NP, 2, NX, NZ), ((0, 4), (2, 16), (3, 4)), -0.2, 0.2)), 0.2, 1.5)
    cont_matrix = normal_values(key_of[4], (CONT, 2 * MATCH), (2 * MATCH) ** -0.5, 1.25, (), jnp.float32)
    fringe_cells = draw_fringe_cells(jax.random.fold_in(key_of[11], 71), 0)
    donor_cells = draw_donor_cells(jax.random.fold_in(key_of[11], 71), 0)
    donor_weights = draw_donor_weights(jax.random.fold_in(key_of[11], 71), 0)
    donor_counts = draw_donor_counts(jax.random.fold_in(key_of[11], 71), 0)
    el_pair = draw_el_pair(jax.random.fold_in(key_of[11], 71), 0)
    ac_pair = draw_ac_pair(jax.random.fold_in(key_of[11], 71), 0)
    return {"elastic": elastic, "acoustic": acoustic, "el_media": el_media, "ac_media": ac_media, "cont_matrix": cont_matrix, "fringe_cells": fringe_cells, "donor_cells": donor_cells, "donor_weights": donor_weights, "donor_counts": donor_counts, "el_pair": el_pair, "ac_pair": ac_pair}


step_size = 0.25
penalty = 2.0


def x_derivative(lines, cont_matrix):
    matching = jnp.concatenate([lines[:, NX - MATCH:, :], lines[:, :MATCH, :]], axis=1)
    tail = jnp.einsum("cg,fgz->fcz", cont_matrix, matching, precision=lax.Precision.HIGHEST)
    extended = jnp.concatenate([lines, tail], axis=1)
    spectrum = jnp.fft.rfft(extended, axis=1)
    modes = jnp.arange(K + 1)
    wavenumber = jnp.where(modes < K, modes * (2.0 * math.pi / P_SIZE), 0.0)
    derived = jnp.fft.irfft(spectrum * (1j * wavenumber)[None, :, None], n=P_SIZE, axis=1)
    return derived[:, :NX, :].astype(lines.dtype)


def z_derivative(fields):
    padded = jnp.pad(fields, ((0, 0), (0, 0), (1, 1)))
    return (padded[:, :, 2:] - padded[:, :, :-2]) * 0.5


def overwrite_fringe(new_field, old_field, fringe_cells, donor_cells, donor_weights, donor_counts):
    recv_index = jnp.arange(NP, dtype=jnp.int32).reshape(NP, 1, 1, 1, 1)
    slab_index = jnp.arange(SLABS, dtype=jnp.int32).reshape(1, SLABS, 1, 1, 1)
    layer_index = jnp.arange(LAYERS, dtype=jnp.int32).reshape(1, 1, LAYERS, 1, 1)
    donor_index = jnp.arange(NP, dtype=jnp.int32).reshape(1, 1, 1, NP, 1)
    donor_x = slab_index[..., None] * XD + donor_cells // ZD
    donor_z = layer_index[..., None] * ZD + donor_cells % ZD
    picked = old_field[donor_index[..., None], :, donor_x, donor_z]
    weights = donor_weights[..., None]
    interp = picked[:, :, :, :, 0] * weights[:, :, :, :, 0]
    interp = interp + picked[:, :, :, :, 1] * weights[:, :, :, :, 1]
    interp = interp + picked[:, :, :, :, 2] * weights[:, :, :, :, 2]
    interp = interp + picked[:, :, :, :, 3] * weights[:, :, :, :, 3]
    fringe_x = slab_index * XD + fringe_cells // ZD
    fringe_z = layer_index * ZD + fringe_cells % ZD
    current = new_field[recv_index, :, fringe_x, fringe_z]
    live = jnp.arange(RCAP, dtype=jnp.int32) < donor_counts[..., None]
    chosen = jnp.where(live[..., None], interp, current)
    return new_field.at[recv_index, :, fringe_x, fringe_z].set(chosen)


def reference(elastic, acoustic, el_media, ac_media, cont_matrix, fringe_cells, donor_cells, donor_weights, donor_counts, el_pair, ac_pair):
    slab_start = (jnp.arange(NX, dtype=jnp.int32) // XD) * XD
    basin_list = []
    ocean_list = []
    for patch_index in range(NP):
        basin = elastic[patch_index]
        ocean = acoustic[patch_index]
        dx_basin = x_derivative(jnp.stack([basin[0], basin[1], basin[2], basin[4]]), cont_matrix)
        dx_ocean = x_derivative(ocean[0:2], cont_matrix)
        depth_diff = z_derivative(jnp.stack([basin[0], basin[1], basin[3], basin[4], ocean[0], ocean[2]]))
        buoyancy = el_media[patch_index, 0]
        lame_first = el_media[patch_index, 1]
        shear_modulus = el_media[patch_index, 2]
        stiffness = lame_first + 2.0 * shear_modulus
        rate_vx = buoyancy * (dx_basin[2] + depth_diff[3])
        rate_vz = buoyancy * (dx_basin[3] + depth_diff[2])
        rate_sxx = stiffness * dx_basin[0] + lame_first * depth_diff[1]
        rate_szz = lame_first * dx_basin[0] + stiffness * depth_diff[1]
        rate_sxz = shear_modulus * (depth_diff[0] + dx_basin[1])
        bulk_modulus = ac_media[patch_index, 0]
        ocean_buoyancy = ac_media[patch_index, 1]
        rate_pressure = -bulk_modulus * (dx_ocean[1] + depth_diff[5])
        rate_ocean_vx = -ocean_buoyancy * dx_ocean[0]
        rate_ocean_vz = -ocean_buoyancy * depth_diff[4]
        pressure_pair = ocean[0][slab_start + el_pair[patch_index], NZ - 1]
        rate_szz = rate_szz.at[:, 0].add(penalty * (-pressure_pair - basin[3][:, 0]))
        velocity_pair = basin[1][slab_start + ac_pair[patch_index], 0]
        rate_ocean_vz = rate_ocean_vz.at[:, NZ - 1].add(penalty * (velocity_pair - ocean[2][:, NZ - 1]))
        basin_rates = jnp.stack([rate_vx, rate_vz, rate_sxx, rate_szz, rate_sxz])
        ocean_rates = jnp.stack([rate_pressure, rate_ocean_vx, rate_ocean_vz])
        basin_list.append(basin + step_size * basin_rates)
        ocean_list.append(ocean + step_size * ocean_rates)
    new_elastic = jnp.stack(basin_list)
    new_acoustic = jnp.stack(ocean_list)
    new_elastic = overwrite_fringe(new_elastic, elastic, fringe_cells, donor_cells, donor_weights, donor_counts)
    new_acoustic = overwrite_fringe(new_acoustic, acoustic, fringe_cells, donor_cells, donor_weights, donor_counts)
    return new_elastic, new_acoustic
```

```python
import functools
import math

import jax
import jax.numpy as jnp
import numpy as np
from jax import lax
from jax.experimental import pallas as pl
from jax.experimental.pallas import tpu as pltpu
from jax.sharding import PartitionSpec as P

P_SIZE = 1152
MATCH = 10
NF = 8
NQ = 4
SL = 64
LANES = 128
MESH_ID = pl.DeviceIdType.MESH
F32 = jnp.float32
BF16 = jnp.bfloat16

EL_OF = {0: 0, 1: 1, 2: 2, 3: 4, 6: 3}
AC_OF = {4: 0, 5: 1, 7: 2}
FED = {0: (2, 6), 1: (3,), 2: (0,), 3: (1,), 4: (5,), 5: (4,)}


def derivative_rows():
    d = np.arange(128)[:, None] - (np.arange(2048)[None, :] - 896)
    d = d % P_SIZE
    angle = np.where(d == 0, 1.0, np.pi * d / P_SIZE)
    value = np.where(d == 0, 0.0, (np.pi / P_SIZE) * np.where(d % 2 == 0, 1.0, -1.0) / np.tan(angle))
    high = value.astype(np.float32).astype(jnp.bfloat16)
    low = (value - high.astype(np.float64)).astype(np.float32).astype(jnp.bfloat16)
    return np.stack([high, low])


def halves(x):
    high = x.astype(BF16)
    low = (x - high.astype(F32)).astype(BF16)
    return high, low


def dot(a, b):
    return jnp.dot(a, b, preferred_element_type=F32)


def exact_dot(a, b):
    return jnp.dot(a, b, preferred_element_type=F32, precision=lax.Precision.HIGHEST)


def lanes_of(shape):
    return lax.broadcasted_iota(jnp.int32, shape, len(shape) - 1)


def rows_of(shape):
    return lax.broadcasted_iota(jnp.int32, shape, len(shape) - 2)


def kernel(
    cnt, el, ac, em, am, cm, fc, dc, dw, elp, acp, wt,
    oel, oac,
    F, H, XF, XP, XB, E, YA, YB, DA, DB, W, CM, FC, PAIR, MEL, MAC,
    RC, RW, VS, VR, S, TH, TL, OH, ACC, SC, MK, HP, HN, O, CO,
    s_load, s_med, s_small, s_fa, r_fa, s_fb, r_fb, s_ra, r_ra, s_rb, r_rb,
    s_rc, r_rc, s_rw, r_rw, s_v, r_v, s_h, r_h, s_out,
):
    me = lax.axis_index("line")
    zc = me // 2
    core = me % 2
    pt = lax.axis_index("patch")
    ly = lax.axis_index("layer")

    def line_of(dz, k):
        return ((zc + dz + 8) % 8) * 2 + k

    loads = {}
    for f in range(NF):
        for q in range(NQ):
            src = el.at[0, EL_OF[f], :, pl.ds(q * LANES, LANES)] if f in EL_OF else ac.at[0, AC_OF[f], :, pl.ds(q * LANES, LANES)]
            loads[f, q] = pltpu.make_async_copy(src, F.at[f, q], s_load.at[f * NQ + q])
            loads[f, q].start()
    small = [
        pltpu.make_async_copy(wt, W, s_small.at[0]),
        pltpu.make_async_copy(cm, CM, s_small.at[1]),
        pltpu.make_async_copy(fc.at[0, 0, 0], FC, s_small.at[2]),
        pltpu.make_async_copy(elp, PAIR.at[0], s_small.at[3]),
        pltpu.make_async_copy(acp, PAIR.at[1], s_small.at[4]),
    ]
    for c in small:
        c.start()
    media = []
    for f in range(3):
        for q in range(NQ):
            media.append(pltpu.make_async_copy(em.at[0, f, :, pl.ds(q * LANES, LANES)], MEL.at[f, q], s_med.at[f * NQ + q]))
    for f in range(2):
        for q in range(NQ):
            media.append(pltpu.make_async_copy(am.at[0, f, :, pl.ds(q * LANES, LANES)], MAC.at[f, q], s_med.at[12 + f * NQ + q]))

    barrier = pltpu.get_barrier_semaphore()
    partners = [{"line": (me + o) % 16} for o in range(1, 16)]
    partners += [{"patch": (pt + o) % 4} for o in range(1, 4)]
    partners += [{"layer": (ly + o) % 4} for o in (1, 3)]
    for p in partners:
        pl.semaphore_signal(barrier, inc=1, device_id=p, device_id_type=MESH_ID)

    for f in range(6):
        for q in range(NQ):
            loads[f, q].wait()
    left64 = lanes_of((32, LANES)) < 64
    for c in range(8):
        t = 3 * c + 1
        top = F[t // 4, t % 4, 0:32]
        bot = F[t // 4, t % 4, 32:64]
        H[2 * c] = jnp.where(left64, top, pltpu.roll(bot, 64, 1))
        H[2 * c + 1] = jnp.where(left64, pltpu.roll(top, 64, 1), bot)
    for f in range(6, 8):
        for q in range(NQ):
            loads[f, q].wait()

    pl.semaphore_wait(barrier, len(partners))

    reqs = []
    for o in range(1, 4):
        q = (pt + o) % 4
        reqs.append(pltpu.make_async_remote_copy(
            src_ref=dc.at[0, 0, 0, q], dst_ref=RC.at[o - 1], send_sem=s_rc.at[o - 1], recv_sem=r_rc.at[o - 1],
            device_id={"patch": q}, device_id_type=MESH_ID))
        reqs.append(pltpu.make_async_remote_copy(
            src_ref=dw.at[0, 0, 0, q], dst_ref=RW.at[o - 1], send_sem=s_rw.at[o - 1], recv_sem=r_rw.at[o - 1],
            device_id={"patch": q}, device_id_type=MESH_ID))
    for r in reqs:
        r.start()
    halo_up = pltpu.make_async_remote_copy(
        src_ref=F.at[:, 0], dst_ref=HN, send_sem=s_h.at[0], recv_sem=r_h.at[0],
        device_id={"layer": (ly + 3) % 4}, device_id_type=MESH_ID)
    halo_down = pltpu.make_async_remote_copy(
        src_ref=F.at[:, 3], dst_ref=HP, send_sem=s_h.at[1], recv_sem=r_h.at[1],
        device_id={"layer": (ly + 1) % 4}, device_id_type=MESH_ID)
    halo_up.start()
    halo_down.start()

    order = [(dz, k) for dz in (4, 3, -3, 2, -2, 1, -1) for k in (0, 1)]
    n_out = len(order)
    other = 1 - core

    def targets():
        for i, (dz, k) in enumerate(order):
            kk = k if i % 2 == k else k
            yield i, (zc + dz + 8) % 8, kk
        yield n_out, zc, other

    def exchange(src_of, dst, send, recv):
        copies = []
        for i, c, k in targets():
            copies.append(pltpu.make_async_remote_copy(
                src_ref=src_of(c, k), dst_ref=dst.at[me], send_sem=send.at[i], recv_sem=recv.at[me],
                device_id={"line": c * 2 + k}, device_id_type=MESH_ID))
        own = pltpu.make_async_copy(src_of(zc, core), dst.at[me], recv.at[me])
        for r in copies:
            r.start()
        own.start()
        return copies

    def full_tile(c, k):
        t = 3 * c + 2 * k
        return F.at[t // 4, t % 4]

    fwd_a = exchange(full_tile, XF, s_fa, r_fa)
    fwd_b = exchange(lambda c, k: H.at[c * 2 + k], XP, s_fb, r_fb)
    for m in media:
        m.start()

    def wait_recv(dst, recv, s):
        pltpu.make_async_copy(dst.at[s], dst.at[s], recv.at[s]).wait()

    for f in range(NF):
        for q in range(NQ):
            hi, lo = halves(F[f, q])
            TH[q * SL:(q + 1) * SL, f * LANES:(f + 1) * LANES] = hi
            TL[q * SL:(q + 1) * SL, f * LANES:(f + 1) * LANES] = lo
    for c in small:
        c.wait()
    S[...] = jnp.zeros_like(S)
    lane_r = lanes_of((256, 256))
    lane_l = lanes_of((256, LANES))
    lane8 = lanes_of((256, LANES))

    def gather(i, carry):
        reqs_c = pltpu.make_async_copy(RC.at[i], RC.at[i], r_rc.at[i])
        reqs_w = pltpu.make_async_copy(RW.at[i], RW.at[i], r_rw.at[i])
        reqs_c.wait()
        reqs_w.wait()
        cells = RC[i]
        S[0:4] = (((cells >> 7) & 3) * SL + (cells >> 9)).astype(F32)
        S[4:8] = (cells & 127).astype(F32)
        S[8:12] = RW[i]
        cols = jnp.transpose(S[...])
        icols = cols.astype(jnp.int32)
        for s in range(4):
            hot = lane_r == icols[:, s:s + 1]
            OH[s * 256:(s + 1) * 256] = jnp.where(hot, 1.0, 0.0).astype(BF16)
        masks = [jnp.where(lane_l == icols[:, 4 + s:5 + s], cols[:, 8 + s:9 + s], 0.0) for s in range(4)]
        for s in range(4):
            ACC[s] = masks[s]
        v = jnp.zeros((256, LANES), F32)
        for fp in range(4):
            th = TH[:, fp * 256:(fp + 1) * 256]
            tl = TL[:, fp * 256:(fp + 1) * 256]
            total = None
            for s in range(4):
                hot = OH[s * 256:(s + 1) * 256]
                g = dot(hot, th) + dot(hot, tl)
                w = ACC[s]
                g = g * jnp.concatenate([w, w], axis=1)
                total = g if total is None else total + g
            for h in range(2):
                one = jnp.sum(total[:, h * LANES:(h + 1) * LANES], axis=1, keepdims=True)
                v = jnp.where(lane8 == fp * 2 + h, one, v)
        VS[i] = jnp.transpose(v)[0:8]
        return carry

    def response(i):
        q = (pt + 3 - i) % 4
        return pltpu.make_async_remote_copy(
            src_ref=VS.at[i], dst_ref=VR.at[i], send_sem=s_v.at[i], recv_sem=r_v.at[i],
            device_id={"patch": q}, device_id_type=MESH_ID)

    lax.fori_loop(0, 3, gather, 0)
    for i in range(3):
        response(i).start()

    def tail_of(last_rows, first_rows):
        E[0:MATCH] = last_rows
        E[MATCH:2 * MATCH] = first_rows
        return exact_dot(CM[...], E[0:2 * MATCH])

    for s in range(16):
        wait_recv(XF, r_fa, s)
    for s in range(16):
        hi, lo = halves(XF[s])
        XB[s * SL:(s + 1) * SL, 0:LANES] = hi
        XB[s * SL:(s + 1) * SL, LANES:] = lo
    hi, lo = halves(tail_of(XF[15, SL - MATCH:], XF[0, 0:MATCH]))
    XB[1024:1152, 0:LANES] = hi
    XB[1024:1152, LANES:] = lo

    def rows_a(step, carry):
        i = (zc + step) % 8
        start = pl.multiple_of((7 - i) * LANES, LANES)
        wh = W[0, :, pl.ds(start, P_SIZE)]
        wl = W[1, :, pl.ds(start, P_SIZE)]
        y = dot(wh, XB[...])
        r = y[:, :LANES] + y[:, LANES:] + dot(wl, XB[:, 0:LANES])
        YA[2 * i] = r[0:SL]
        YA[2 * i + 1] = r[SL:]
        return carry

    lax.fori_loop(0, 8, rows_a, 0)
    ret_a = exchange(lambda c, k: YA.at[c * 2 + k], DA, s_ra, r_ra)

    for i in range(3):
        wait_recv(VR, r_v, i)
    S[...] = jnp.zeros_like(S)
    row_r = rows_of((256, 256))
    slot = rows_of((256, LANES))
    for i in range(3):
        q = (pt + i + 1) % 4
        cells = FC[pl.ds(q, 1)]
        S[0:8] = VR[i]
        S[8:9] = (cells & 127).astype(F32)
        cols = jnp.transpose(S[...])
        target = ((cells >> 7) & 3) * SL + (cells >> 9)
        hot = jnp.where(row_r == target, 1.0, 0.0).astype(BF16)
        live = (lane_l == cols[:, 8:9].astype(jnp.int32)) & (slot < cnt[0, 0, 0, q])
        livef = jnp.where(live, 1.0, 0.0)
        part = dot(hot, livef.astype(BF16))
        MK[...] = part if i == 0 else MK[...] + part
        for fp in range(4):
            b = jnp.concatenate([livef * cols[:, 2 * fp:2 * fp + 1], livef * cols[:, 2 * fp + 1:2 * fp + 2]], axis=1)
            hi, lo = halves(b)
            part = dot(hot, hi) + dot(hot, lo)
            SC[fp] = part if i == 0 else SC[fp] + part

    for s in range(16):
        wait_recv(XP, r_fb, s)
    left = lanes_of((SL, LANES)) < 64

    def spread(s):
        x = XP[s]
        r = pltpu.roll(x, 64, 1)
        return jnp.where(left64, x, r), jnp.where(left64, r, x)

    def store_b(at, x):
        hi, lo = halves(x)
        keep = lanes_of(x.shape) < 64
        XB[at:at + x.shape[0], 0:LANES] = jnp.where(keep, hi.astype(F32), lo.astype(F32)).astype(BF16)

    ends = {}
    for s in range(16):
        a, b = spread(s)
        store_b(s * SL, a)
        store_b(s * SL + 32, b)
        if s == 0:
            E[MATCH:2 * MATCH] = a[0:MATCH]
        if s == 15:
            E[0:MATCH] = b[32 - MATCH:]
    store_b(1024, exact_dot(CM[...], E[0:2 * MATCH]))

    def rows_b(step, carry):
        i = (zc + step) % 8
        start = pl.multiple_of((7 - i) * LANES, LANES)
        x = XB[:, 0:LANES]
        y = dot(W[0, :, pl.ds(start, P_SIZE)], x) + dot(W[1, :, pl.ds(start, P_SIZE)], x)
        r = y + pltpu.roll(y, 64, 1)
        YB[2 * i] = jnp.where(left64, r[0:32], r[32:64])
        YB[2 * i + 1] = jnp.where(left64, r[64:96], r[96:128])
        return carry

    lax.fori_loop(0, 8, rows_b, 0)
    ret_b = exchange(lambda c, k: YB.at[c * 2 + k], DB, s_rb, r_rb)

    pltpu.make_async_copy(HN, HN, r_h.at[0]).wait()
    pltpu.make_async_copy(HP, HP, r_h.at[1]).wait()
    for m in media:
        m.wait()
    lane = lanes_of((SL, LANES))
    first = ly == 0
    last = ly == 3
    S[...] = jnp.zeros_like(S)
    S[0:1, 0:64] = PAIR[0].astype(F32)
    S[1:2, 0:64] = PAIR[1].astype(F32)
    pair_cols = jnp.transpose(S[:, 0:LANES]).astype(jnp.int32)
    lane64 = lanes_of((SL, SL))
    pick_el = jnp.where(lane64 == pair_cols[0:64, 0:1], 1.0, 0.0)
    pick_ac = jnp.where(lane64 == pair_cols[0:64, 1:2], 1.0, 0.0)
    pressure = pltpu.roll(exact_dot(pick_el, HP[4]), 1, 1)
    velocity = pltpu.roll(exact_dot(pick_ac, HN[1]), LANES - 1, 1)
    zero_first = jnp.where(first, 0.0, 1.0)
    zero_last = jnp.where(last, 0.0, 1.0)
    one_first = jnp.where(first, 1.0, 0.0)
    one_last = jnp.where(last, 1.0, 0.0)

    for q in range(NQ):
        def dz(f):
            cur = F[f, q]
            prev = F[f, q - 1] if q else HP[f] * zero_first
            nxt = F[f, q + 1] if q < 3 else HN[f] * zero_last
            below = jnp.where(lane == LANES - 1, pltpu.roll(nxt, LANES - 1, 1), pltpu.roll(cur, LANES - 1, 1))
            above = jnp.where(lane == 0, pltpu.roll(prev, 1, 1), pltpu.roll(cur, 1, 1))
            return (below - above) * 0.125

        buoy, lam, mu = MEL[0, q], MEL[1, q], MEL[2, q]
        stiff = lam + 2.0 * mu
        bulk, obuoy = MAC[0, q], MAC[1, q]
        mask = MK[q * SL:(q + 1) * SL] > 0.5

        def put(f, base, coef):
            scat = SC[f // 2, q * SL:(q + 1) * SL, (f % 2) * LANES:(f % 2 + 1) * LANES]
            O[f, q] = jnp.where(mask, scat, base)
            if coef is not None:
                CO[f, q] = jnp.where(mask, 0.0, 0.25 * coef)

        dvz = dz(1)
        put(0, F[0, q] + buoy * dz(3), buoy)
        put(1, F[1, q] + buoy * dz(6), buoy)
        put(2, F[2, q] + lam * dvz, stiff)
        szz = F[6, q] + stiff * dvz
        if q == 0:
            szz = szz + jnp.where(lane == 0, one_first * 0.5 * (-pressure - F[6, q]), 0.0)
        put(6, szz, lam)
        put(3, F[3, q] + mu * dz(0), mu)
        put(4, F[4, q] - bulk * dz(7), -bulk)
        put(5, F[5, q], -obuoy)
        ovz = F[7, q] - obuoy * dz(4)
        if q == 3:
            ovz = ovz + jnp.where(lane == LANES - 1, one_last * 0.5 * (velocity - F[7, q]), 0.0)
        put(7, ovz, None)

    outs = []

    def emit(f, q):
        dst = oel.at[0, EL_OF[f], :, pl.ds(q * LANES, LANES)] if f in EL_OF else oac.at[0, AC_OF[f], :, pl.ds(q * LANES, LANES)]
        c = pltpu.make_async_copy(O.at[f, q], dst, s_out.at[f * NQ + q])
        c.start()
        outs.append(c)

    for q in range(NQ):
        emit(7, q)

    def finish(t, dx):
        f, q = t // 4, t % 4
        for g in FED[f]:
            O[g, q] = O[g, q] + CO[g, q] * dx
            emit(g, q)

    for c in range(8):
        for k in range(2):
            wait_recv(DA, r_ra, 2 * c + k)
            finish(3 * c + 2 * k, DA[2 * c + k])
    for c in range(8):
        wait_recv(DB, r_rb, 2 * c)
        wait_recv(DB, r_rb, 2 * c + 1)
        pa, pb = DB[2 * c], DB[2 * c + 1]
        top = jnp.where(left64, pa, pltpu.roll(pb, 64, 1))
        bot = jnp.where(left64, pltpu.roll(pa, 64, 1), pb)
        finish(3 * c + 1, jnp.concatenate([top, bot], axis=0))

    for r in reqs:
        r.wait_send()
    for i in range(3):
        response(i).wait_send()
    halo_up.wait_send()
    halo_down.wait_send()
    for group in (fwd_a, fwd_b, ret_a, ret_b):
        for r in group:
            r.wait_send()
    for c in outs:
        c.wait()


def per_device(elastic, acoustic, el_media, ac_media, cont_matrix, fringe_cells, donor_cells, donor_weights, donor_counts, el_pair, ac_pair):
    anywhere = pl.BlockSpec(memory_space=pl.ANY)
    vm = pltpu.VMEM
    dma = pltpu.SemaphoreType.DMA
    scratch = [
        vm((NF, NQ, SL, LANES), F32),
        vm((16, 32, LANES), F32),
        vm((16, SL, LANES), F32),
        vm((16, 32, LANES), F32),
        vm((P_SIZE, 256), BF16),
        vm((32, LANES), F32),
        vm((16, SL, LANES), F32),
        vm((16, 32, LANES), F32),
        vm((16, SL, LANES), F32),
        vm((16, 32, LANES), F32),
        vm((2, 128, 2048), BF16),
        vm((128, 2 * MATCH), F32),
        vm((4, 256), jnp.int32),
        vm((2, 1, 64), jnp.int32),
        vm((3, NQ, SL, LANES), F32),
        vm((2, NQ, SL, LANES), F32),
        vm((3, 4, 256), jnp.int32),
        vm((3, 4, 256), F32),
        vm((3, 8, 256), F32),
        vm((3, 8, 256), F32),
        vm((LANES, 256), F32),
        vm((256, 1024), BF16),
        vm((256, 1024), BF16),
        vm((1024, 256), BF16),
        vm((4, 256, LANES), F32),
        vm((4, 256, 256), F32),
        vm((256, LANES), F32),
        vm((NF, SL, LANES), F32),
        vm((NF, SL, LANES), F32),
        vm((NF, NQ, SL, LANES), F32),
        vm((7, NQ, SL, LANES), F32),
        dma((32,)), dma((20,)), dma((5,)),
        dma((15,)), dma((16,)), dma((15,)), dma((16,)),
        dma((15,)), dma((16,)), dma((15,)), dma((16,)),
        dma((3,)), dma((3,)), dma((3,)), dma((3,)), dma((3,)), dma((3,)),
        dma((2,)), dma((2,)), dma((32,)),
    ]
    call = pl.pallas_call(
        kernel,
        out_shape=(jax.ShapeDtypeStruct(elastic.shape, F32), jax.ShapeDtypeStruct(acoustic.shape, F32)),
        in_specs=[pl.BlockSpec(memory_space=pltpu.SMEM)] + [anywhere] * 11,
        out_specs=(anywhere, anywhere),
        scratch_shapes=scratch,
        compiler_params=pltpu.CompilerParams(collective_id=0, has_side_effects=True),
    )
    return call(
        donor_counts, elastic, acoustic, el_media, ac_media, cont_matrix,
        fringe_cells, donor_cells, donor_weights, el_pair, ac_pair, jnp.asarray(derivative_rows()),
    )


def solution(mesh):
    fields = P("patch", None, "line", "layer")
    placed = (
        fields, fields, fields, fields,
        P(),
        P("patch", "line", "layer", None, None),
        P("patch", "line", "layer", None, None, None),
        P("patch", "line", "layer", None, None, None),
        P("patch", "line", "layer", None),
        P("patch", "line"),
        P("patch", "line"),
    )
    return jax.shard_map(per_device, mesh=mesh, in_specs=placed, out_specs=(fields, fields), check_vma=False)
```

```python
import functools
import math

import jax
import jax.numpy as jnp
import numpy as np
from jax import lax
from jax.experimental import pallas as pl
from jax.experimental.pallas import tpu as pltpu
from jax.sharding import PartitionSpec as P

P_SIZE = 1152
MATCH = 10
NF = 8
NQ = 4
SL = 64
LANES = 128
MESH_ID = pl.DeviceIdType.MESH
F32 = jnp.float32
BF16 = jnp.bfloat16

EL_OF = {0: 0, 1: 1, 2: 2, 3: 4, 6: 3}
AC_OF = {4: 0, 5: 1, 7: 2}
FED = {0: (2, 6), 1: (3,), 2: (0,), 3: (1,), 4: (5,), 5: (4,)}


def derivative_rows():
    d = np.arange(128)[:, None] - (np.arange(2048)[None, :] - 896)
    d = d % P_SIZE
    angle = np.where(d == 0, 1.0, np.pi * d / P_SIZE)
    value = np.where(d == 0, 0.0, (np.pi / P_SIZE) * np.where(d % 2 == 0, 1.0, -1.0) / np.tan(angle))
    high = value.astype(np.float32).astype(jnp.bfloat16)
    low = (value - high.astype(np.float64)).astype(np.float32).astype(jnp.bfloat16)
    return np.stack([high, low])


def halves(x):
    high = x.astype(BF16)
    low = (x - high.astype(F32)).astype(BF16)
    return high, low


def dot(a, b):
    return jnp.dot(a, b, preferred_element_type=F32)


def exact_dot(a, b):
    return jnp.dot(a, b, preferred_element_type=F32, precision=lax.Precision.HIGHEST)


def lanes_of(shape):
    return lax.broadcasted_iota(jnp.int32, shape, len(shape) - 1)


def rows_of(shape):
    return lax.broadcasted_iota(jnp.int32, shape, len(shape) - 2)


def kernel(
    cnt, el, ac, em, am, cm, fc, dc, dw, elp, acp, wt,
    oel, oac,
    F, H, XF, XP, XB, E, YA, YB, DA, DB, W, CM, C128, FC, PAIR, MEL, MAC,
    RC, RW, VS, VR, S, TH, TL, OH, ACC, SC, MK, HP, HN, CO,
    s_load, s_med, s_small, s_fa, r_fa, s_fb, r_fb, s_ra, r_ra, s_rb, r_rb,
    s_rc, r_rc, s_rw, r_rw, s_v, r_v, s_h, r_h,
):
    me = lax.axis_index("line")
    zc = me // 2
    core = me % 2
    pt = lax.axis_index("patch")
    ly = lax.axis_index("layer")

    def line_of(dz, k):
        return ((zc + dz + 8) % 8) * 2 + k

    def out_of(f, q):
        cols = slice(q * LANES, (q + 1) * LANES)
        return (oel, (0, EL_OF[f], slice(None), cols)) if f in EL_OF else (oac, (0, AC_OF[f], slice(None), cols))

    barrier = pltpu.get_barrier_semaphore()
    partners = [{"line": (me + o) % 16} for o in range(1, 16)]
    partners += [{"patch": (pt + o) % 4} for o in range(1, 4)]
    partners += [{"layer": (ly + o) % 4} for o in (1, 3)]
    for p in partners:
        pl.semaphore_signal(barrier, inc=1, device_id=p, device_id_type=MESH_ID)

    loads = {}
    for f in range(NF):
        for q in range(NQ):
            src = el.at[0, EL_OF[f], :, pl.ds(q * LANES, LANES)] if f in EL_OF else ac.at[0, AC_OF[f], :, pl.ds(q * LANES, LANES)]
            loads[f, q] = pltpu.make_async_copy(src, F.at[f, q], s_load.at[f * NQ + q])
            loads[f, q].start()
    small = [
        pltpu.make_async_copy(wt, W, s_small.at[0]),
        pltpu.make_async_copy(cm, CM, s_small.at[1]),
        pltpu.make_async_copy(fc.at[0, 0, 0], FC, s_small.at[2]),
        pltpu.make_async_copy(elp, PAIR.at[0], s_small.at[3]),
        pltpu.make_async_copy(acp, PAIR.at[1], s_small.at[4]),
    ]
    for c in small:
        c.start()
    media = []
    for f in range(3):
        for q in range(NQ):
            media.append(pltpu.make_async_copy(em.at[0, f, :, pl.ds(q * LANES, LANES)], MEL.at[f, q], s_med.at[f * NQ + q]))
    for f in range(2):
        for q in range(NQ):
            media.append(pltpu.make_async_copy(am.at[0, f, :, pl.ds(q * LANES, LANES)], MAC.at[f, q], s_med.at[12 + f * NQ + q]))

    for f in range(6):
        for q in range(NQ):
            loads[f, q].wait()
    for f in range(6, 8):
        for q in range(NQ):
            loads[f, q].wait()

    pl.semaphore_wait(barrier, len(partners))

    reqs = []
    for o in range(1, 4):
        q = (pt + o) % 4
        reqs.append(pltpu.make_async_remote_copy(
            src_ref=dc.at[0, 0, 0, q], dst_ref=RC.at[o - 1], send_sem=s_rc.at[o - 1], recv_sem=r_rc.at[o - 1],
            device_id={"patch": q}, device_id_type=MESH_ID))
        reqs.append(pltpu.make_async_remote_copy(
            src_ref=dw.at[0, 0, 0, q], dst_ref=RW.at[o - 1], send_sem=s_rw.at[o - 1], recv_sem=r_rw.at[o - 1],
            device_id={"patch": q}, device_id_type=MESH_ID))
    for r in reqs:
        r.start()
    halo_up = pltpu.make_async_remote_copy(
        src_ref=F.at[:, 0], dst_ref=HN, send_sem=s_h.at[0], recv_sem=r_h.at[0],
        device_id={"layer": (ly + 3) % 4}, device_id_type=MESH_ID)
    halo_down = pltpu.make_async_remote_copy(
        src_ref=F.at[:, 3], dst_ref=HP, send_sem=s_h.at[1], recv_sem=r_h.at[1],
        device_id={"layer": (ly + 1) % 4}, device_id_type=MESH_ID)
    halo_up.start()
    halo_down.start()

    order = [(dz, k) for dz in (4, 3, -3, 2, -2, 1, -1) for k in (0, 1)]
    n_out = len(order)
    other = 1 - core

    def targets():
        for i, (dz, k) in enumerate(order):
            yield i, (zc + dz + 8) % 8, k
        yield n_out, zc, other

    def exchange(src_of, dst, send, recv):
        copies = []
        for i, c, k in targets():
            copies.append(pltpu.make_async_remote_copy(
                src_ref=src_of(c, k), dst_ref=dst.at[me], send_sem=send.at[i], recv_sem=recv.at[me],
                device_id={"line": c * 2 + k}, device_id_type=MESH_ID))
        own = pltpu.make_async_copy(src_of(zc, core), dst.at[me], recv.at[me])
        for r in copies:
            r.start()
        own.start()
        return copies

    def full_tile(c, k):
        t = 3 * c + 2 * k
        return F.at[t // 4, t % 4]

    fwd_a = exchange(full_tile, XF, s_fa, r_fa)
    left64 = lanes_of((32, LANES)) < 64
    for c in range(8):
        t = 3 * c + 1
        top = F[t // 4, t % 4, 0:32]
        bot = F[t // 4, t % 4, 32:64]
        H[2 * c] = jnp.where(left64, top, pltpu.roll(bot, 64, 1))
        H[2 * c + 1] = jnp.where(left64, pltpu.roll(top, 64, 1), bot)
    for m in media:
        m.start()

    def wait_recv(dst, recv, s):
        pltpu.make_async_copy(dst.at[s], dst.at[s], recv.at[s]).wait()

    for f in range(NF):
        for q in range(NQ):
            hi, lo = halves(F[f, q])
            TH[q * SL:(q + 1) * SL, f * LANES:(f + 1) * LANES] = hi
            TL[q * SL:(q + 1) * SL, f * LANES:(f + 1) * LANES] = lo
    fwd_b = exchange(lambda c, k: H.at[c * 2 + k], XP, s_fb, r_fb)
    for c in small:
        c.wait()
    S[...] = jnp.zeros_like(S)
    S[0:2 * MATCH] = jnp.concatenate([CM[...], CM[...]], axis=1)
    C128[...] = jnp.transpose(S[...])[0:LANES]
    E[...] = jnp.zeros_like(E)
    S[...] = jnp.zeros_like(S)
    lane_r = lanes_of((256, 256))
    lane_l = lanes_of((256, LANES))
    lane8 = lanes_of((256, LANES))

    def gather(i, carry):
        reqs_c = pltpu.make_async_copy(RC.at[i], RC.at[i], r_rc.at[i])
        reqs_w = pltpu.make_async_copy(RW.at[i], RW.at[i], r_rw.at[i])
        reqs_c.wait()
        reqs_w.wait()
        cells = RC[i]
        S[0:4] = (((cells >> 7) & 3) * SL + (cells >> 9)).astype(F32)
        S[4:8] = (cells & 127).astype(F32)
        S[8:12] = RW[i]
        cols = jnp.transpose(S[...])
        icols = cols.astype(jnp.int32)
        for s in range(4):
            hot = lane_r == icols[:, s:s + 1]
            OH[s * 256:(s + 1) * 256] = jnp.where(hot, 1.0, 0.0).astype(BF16)
        masks = [jnp.where(lane_l == icols[:, 4 + s:5 + s], cols[:, 8 + s:9 + s], 0.0) for s in range(4)]
        for s in range(4):
            ACC[s] = masks[s]
        v = jnp.zeros((256, LANES), F32)
        for fp in range(4):
            th = TH[:, fp * 256:(fp + 1) * 256]
            tl = TL[:, fp * 256:(fp + 1) * 256]
            total = None
            for s in range(4):
                hot = OH[s * 256:(s + 1) * 256]
                g = dot(hot, th) + dot(hot, tl)
                w = ACC[s]
                g = g * jnp.concatenate([w, w], axis=1)
                total = g if total is None else total + g
            for h in range(2):
                one = jnp.sum(total[:, h * LANES:(h + 1) * LANES], axis=1, keepdims=True)
                v = jnp.where(lane8 == fp * 2 + h, one, v)
        VS[i] = jnp.transpose(v)[0:8]
        return carry

    def response(i):
        q = (pt + 3 - i) % 4
        return pltpu.make_async_remote_copy(
            src_ref=VS.at[i], dst_ref=VR.at[i], send_sem=s_v.at[i], recv_sem=r_v.at[i],
            device_id={"patch": q}, device_id_type=MESH_ID)

    lax.fori_loop(0, 3, gather, 0)
    for i in range(3):
        response(i).start()

    def far_first(step):
        return ((8 - step) // 2) * (2 * (step % 2) - 1)

    arrivals = [(zc, core), (zc, other)] + [((zc + dz + 8) % 8, k) for dz in (1, -1, 2, -2, 3, -3, 4) for k in (0, 1)]

    def send_block(step, src, dst, send, recv):
        c = (zc + far_first(step) + 8) % 8
        for k in range(2):
            pltpu.make_async_remote_copy(
                src_ref=src.at[2 * c + k], dst_ref=dst.at[me], send_sem=send.at[2 * step + k], recv_sem=recv.at[me],
                device_id={"line": 2 * c + k}, device_id_type=MESH_ID).start()

    def send_last(src, dst, send, recv):
        pltpu.make_async_remote_copy(
            src_ref=src.at[2 * zc + other], dst_ref=dst.at[me], send_sem=send.at[14], recv_sem=recv.at[me],
            device_id={"line": 2 * zc + other}, device_id_type=MESH_ID).start()
        pltpu.make_async_copy(src.at[me], dst.at[me], recv.at[me]).start()

    def wait_sent(src, dst, send, recv):
        for i in range(15):
            pltpu.make_async_remote_copy(
                src_ref=src.at[0], dst_ref=dst.at[0], send_sem=send.at[i], recv_sem=recv.at[0],
                device_id={"line": 2 * zc + other}, device_id_type=MESH_ID).wait_send()

    def store_a(at, x):
        hi, lo = halves(x)
        XB[pl.ds(at, x.shape[0]), 0:LANES] = hi
        XB[pl.ds(at, x.shape[0]), LANES:] = lo

    for c, k in arrivals:
        s = 2 * c + k
        wait_recv(XF, r_fa, s)
        store_a(pl.multiple_of(s * SL, SL), XF[s])
    E[0:MATCH] = XF[15, SL - MATCH:]
    E[MATCH:2 * MATCH] = XF[0, 0:MATCH]
    store_a(1024, exact_dot(C128[...], E[...]))

    def rows_a(step, carry):
        i = (zc + far_first(step) + 8) % 8
        start = pl.multiple_of((7 - i) * LANES, LANES)
        wh = W[0, :, pl.ds(start, P_SIZE)]
        wl = W[1, :, pl.ds(start, P_SIZE)]
        y = dot(wh, XB[...])
        r = y[:, :LANES] + y[:, LANES:] + dot(wl, XB[:, 0:LANES])
        YA[2 * i] = r[0:SL]
        YA[2 * i + 1] = r[SL:]

        @pl.when(step > 0)
        def _():
            send_block(step - 1, YA, DA, s_ra, r_ra)

        return carry

    lax.fori_loop(0, 8, rows_a, 0)
    send_last(YA, DA, s_ra, r_ra)

    for i in range(3):
        wait_recv(VR, r_v, i)
    S[...] = jnp.zeros_like(S)
    row_r = rows_of((256, 256))
    slot = rows_of((256, LANES))
    for i in range(3):
        q = (pt + i + 1) % 4
        cells = FC[pl.ds(q, 1)]
        S[0:8] = VR[i]
        S[8:9] = (cells & 127).astype(F32)
        cols = jnp.transpose(S[...])
        target = ((cells >> 7) & 3) * SL + (cells >> 9)
        hot = jnp.where(row_r == target, 1.0, 0.0).astype(BF16)
        live = (lane_l == cols[:, 8:9].astype(jnp.int32)) & (slot < cnt[0, 0, 0, q])
        livef = jnp.where(live, 1.0, 0.0)
        part = dot(hot, livef.astype(BF16))
        MK[...] = part if i == 0 else MK[...] + part
        for fp in range(4):
            b = jnp.concatenate([livef * cols[:, 2 * fp:2 * fp + 1], livef * cols[:, 2 * fp + 1:2 * fp + 2]], axis=1)
            hi, lo = halves(b)
            part = dot(hot, hi) + dot(hot, lo)
            SC[fp] = part if i == 0 else SC[fp] + part

    def spread(x):
        r = pltpu.roll(x, 64, 1)
        return jnp.where(left64, x, r), jnp.where(left64, r, x)

    def store_b(at, x):
        hi, lo = halves(x)
        keep = lanes_of(x.shape) < 64
        XB[pl.ds(at, x.shape[0]), 0:LANES] = jnp.where(keep, hi.astype(F32), lo.astype(F32)).astype(BF16)

    for c, k in arrivals:
        s = 2 * c + k
        wait_recv(XP, r_fb, s)
        a, b = spread(XP[s])
        store_b(pl.multiple_of(s * SL, SL), a)
        store_b(pl.multiple_of(s * SL + 32, 32), b)
    E[0:MATCH] = spread(XP[15])[1][32 - MATCH:]
    E[MATCH:2 * MATCH] = spread(XP[0])[0][0:MATCH]
    store_b(1024, exact_dot(C128[...], E[...]))

    def rows_b(step, carry):
        i = (zc + far_first(step) + 8) % 8
        start = pl.multiple_of((7 - i) * LANES, LANES)
        x = XB[:, 0:LANES]
        y = dot(W[0, :, pl.ds(start, P_SIZE)], x) + dot(W[1, :, pl.ds(start, P_SIZE)], x)
        r = y + pltpu.roll(y, 64, 1)
        YB[2 * i] = jnp.where(left64, r[0:32], r[32:64])
        YB[2 * i + 1] = jnp.where(left64, r[64:96], r[96:128])

        @pl.when(step > 0)
        def _():
            send_block(step - 1, YB, DB, s_rb, r_rb)

        return carry

    lax.fori_loop(0, 8, rows_b, 0)
    send_last(YB, DB, s_rb, r_rb)

    pltpu.make_async_copy(HN, HN, r_h.at[0]).wait()
    pltpu.make_async_copy(HP, HP, r_h.at[1]).wait()
    for m in media:
        m.wait()
    lane = lanes_of((SL, LANES))
    first = ly == 0
    last = ly == 3
    S[...] = jnp.zeros_like(S)
    S[0:1, 0:64] = PAIR[0].astype(F32)
    S[1:2, 0:64] = PAIR[1].astype(F32)
    pair_cols = jnp.transpose(S[:, 0:LANES]).astype(jnp.int32)
    lane64 = lanes_of((SL, SL))
    pick_el = jnp.where(lane64 == pair_cols[0:64, 0:1], 1.0, 0.0)
    pick_ac = jnp.where(lane64 == pair_cols[0:64, 1:2], 1.0, 0.0)
    pressure = pltpu.roll(exact_dot(pick_el, HP[4]), 1, 1)
    velocity = pltpu.roll(exact_dot(pick_ac, HN[1]), LANES - 1, 1)
    zero_first = jnp.where(first, 0.0, 1.0)
    zero_last = jnp.where(last, 0.0, 1.0)
    one_first = jnp.where(first, 1.0, 0.0)
    one_last = jnp.where(last, 1.0, 0.0)

    for q in range(NQ):
        def dz(f):
            cur = F[f, q]
            prev = F[f, q - 1] if q else HP[f] * zero_first
            nxt = F[f, q + 1] if q < 3 else HN[f] * zero_last
            below = jnp.where(lane == LANES - 1, pltpu.roll(nxt, LANES - 1, 1), pltpu.roll(cur, LANES - 1, 1))
            above = jnp.where(lane == 0, pltpu.roll(prev, 1, 1), pltpu.roll(cur, 1, 1))
            return (below - above) * 0.125

        buoy, lam, mu = MEL[0, q], MEL[1, q], MEL[2, q]
        stiff = lam + 2.0 * mu
        bulk, obuoy = MAC[0, q], MAC[1, q]
        mask = MK[q * SL:(q + 1) * SL] > 0.5

        def put(f, base, coef):
            scat = SC[f // 2, q * SL:(q + 1) * SL, (f % 2) * LANES:(f % 2 + 1) * LANES]
            ref, at = out_of(f, q)
            ref[at] = jnp.where(mask, scat, base)
            if coef is not None:
                CO[f, q] = jnp.where(mask, 0.0, 0.25 * coef)

        dvz = dz(1)
        put(0, F[0, q] + buoy * dz(3), buoy)
        put(1, F[1, q] + buoy * dz(6), buoy)
        put(2, F[2, q] + lam * dvz, stiff)
        szz = F[6, q] + stiff * dvz
        if q == 0:
            szz = szz + jnp.where(lane == 0, one_first * 0.5 * (-pressure - F[6, q]), 0.0)
        put(6, szz, lam)
        put(3, F[3, q] + mu * dz(0), mu)
        put(4, F[4, q] - bulk * dz(7), -bulk)
        put(5, F[5, q], -obuoy)
        ovz = F[7, q] - obuoy * dz(4)
        if q == 3:
            ovz = ovz + jnp.where(lane == LANES - 1, one_last * 0.5 * (velocity - F[7, q]), 0.0)
        put(7, ovz, None)

    def finish(t, dx):
        f, q = t // 4, t % 4
        for g in FED[f]:
            ref, at = out_of(g, q)
            ref[at] = ref[at] + CO[g, q] * dx

    for c in range(8):
        for k in range(2):
            wait_recv(DA, r_ra, 2 * c + k)
            finish(3 * c + 2 * k, DA[2 * c + k])
    for c in range(8):
        wait_recv(DB, r_rb, 2 * c)
        wait_recv(DB, r_rb, 2 * c + 1)
        pa, pb = DB[2 * c], DB[2 * c + 1]
        top = jnp.where(left64, pa, pltpu.roll(pb, 64, 1))
        bot = jnp.where(left64, pltpu.roll(pa, 64, 1), pb)
        finish(3 * c + 1, jnp.concatenate([top, bot], axis=0))

    for r in reqs:
        r.wait_send()
    for i in range(3):
        response(i).wait_send()
    halo_up.wait_send()
    halo_down.wait_send()
    for group in (fwd_a, fwd_b):
        for r in group:
            r.wait_send()
    wait_sent(YA, DA, s_ra, r_ra)
    wait_sent(YB, DB, s_rb, r_rb)


def per_device(elastic, acoustic, el_media, ac_media, cont_matrix, fringe_cells, donor_cells, donor_weights, donor_counts, el_pair, ac_pair):
    anywhere = pl.BlockSpec(memory_space=pl.ANY)
    vm = pltpu.VMEM
    dma = pltpu.SemaphoreType.DMA
    scratch = [
        vm((NF, NQ, SL, LANES), F32),
        vm((16, 32, LANES), F32),
        vm((16, SL, LANES), F32),
        vm((16, 32, LANES), F32),
        vm((P_SIZE, 256), BF16),
        vm((LANES, LANES), F32),
        vm((16, SL, LANES), F32),
        vm((16, 32, LANES), F32),
        vm((16, SL, LANES), F32),
        vm((16, 32, LANES), F32),
        vm((2, 128, 2048), BF16),
        vm((2 * MATCH, 128), F32),
        vm((LANES, LANES), F32),
        vm((4, 256), jnp.int32),
        vm((2, 1, 64), jnp.int32),
        vm((3, NQ, SL, LANES), F32),
        vm((2, NQ, SL, LANES), F32),
        vm((3, 4, 256), jnp.int32),
        vm((3, 4, 256), F32),
        vm((3, 8, 256), F32),
        vm((3, 8, 256), F32),
        vm((LANES, 256), F32),
        vm((256, 1024), BF16),
        vm((256, 1024), BF16),
        vm((1024, 256), BF16),
        vm((4, 256, LANES), F32),
        vm((4, 256, 256), F32),
        vm((256, LANES), F32),
        vm((NF, SL, LANES), F32),
        vm((NF, SL, LANES), F32),
        vm((7, NQ, SL, LANES), F32),
        dma((32,)), dma((20,)), dma((5,)),
        dma((15,)), dma((16,)), dma((15,)), dma((16,)),
        dma((15,)), dma((16,)), dma((15,)), dma((16,)),
        dma((3,)), dma((3,)), dma((3,)), dma((3,)), dma((3,)), dma((3,)),
        dma((2,)), dma((2,)),
    ]
    call = pl.pallas_call(
        kernel,
        out_shape=(pltpu.VMEM(elastic.shape, F32), pltpu.VMEM(acoustic.shape, F32)),
        in_specs=[pl.BlockSpec(memory_space=pltpu.SMEM)] + [anywhere] * 11,
        out_specs=(pl.BlockSpec(memory_space=pltpu.VMEM),) * 2,
        scratch_shapes=scratch,
        compiler_params=pltpu.CompilerParams(collective_id=0, has_side_effects=True),
    )
    return call(
        donor_counts, elastic, acoustic, el_media, ac_media, cont_matrix.T,
        fringe_cells, donor_cells, donor_weights, el_pair, ac_pair, jnp.asarray(derivative_rows()),
    )


def solution(mesh):
    fields = P("patch", None, "line", "layer")
    placed = (
        fields, fields, fields, fields,
        P(),
        P("patch", "line", "layer", None, None),
        P("patch", "line", "layer", None, None, None),
        P("patch", "line", "layer", None, None, None),
        P("patch", "line", "layer", None),
        P("patch", "line"),
        P("patch", "line"),
    )
    return jax.shard_map(per_device, mesh=mesh, in_specs=placed, out_specs=(fields, fields), check_vma=False)
```

```python
import functools
import math

import jax
import jax.numpy as jnp
import numpy as np
from jax import lax
from jax.experimental import pallas as pl
from jax.experimental.pallas import tpu as pltpu
from jax.sharding import PartitionSpec as P

P_SIZE = 1152
MATCH = 10
NF = 8
NQ = 4
SL = 64
LANES = 128
MESH_ID = pl.DeviceIdType.MESH
F32 = jnp.float32
BF16 = jnp.bfloat16

EL_OF = {0: 0, 1: 1, 2: 2, 3: 4, 6: 3}
AC_OF = {4: 0, 5: 1, 7: 2}
FED = {0: (2, 6), 1: (3,), 2: (0,), 3: (1,), 4: (5,), 5: (4,)}


def derivative_rows():
    d = np.arange(128)[:, None] - (np.arange(2048)[None, :] - 896)
    d = d % P_SIZE
    angle = np.where(d == 0, 1.0, np.pi * d / P_SIZE)
    value = np.where(d == 0, 0.0, (np.pi / P_SIZE) * np.where(d % 2 == 0, 1.0, -1.0) / np.tan(angle))
    high = value.astype(np.float32).astype(jnp.bfloat16)
    low = (value - high.astype(np.float64)).astype(np.float32).astype(jnp.bfloat16)
    return np.stack([high, low])


def halves(x):
    high = x.astype(BF16)
    low = (x - high.astype(F32)).astype(BF16)
    return high, low


def dot(a, b):
    return jnp.dot(a, b, preferred_element_type=F32)


def exact_dot(a, b):
    return jnp.dot(a, b, preferred_element_type=F32, precision=lax.Precision.HIGHEST)


def lanes_of(shape):
    return lax.broadcasted_iota(jnp.int32, shape, len(shape) - 1)


def rows_of(shape):
    return lax.broadcasted_iota(jnp.int32, shape, len(shape) - 2)


def tile_of(oel, oac, f, q):
    cols = pl.ds(q * LANES, LANES)
    return oel.at[0, EL_OF[f], :, cols] if f in EL_OF else oac.at[0, AC_OF[f], :, cols]


def finish(bel, bac, CO, DA, DB, oel, oac, O, sem):
    left64 = lanes_of((32, LANES)) < 64
    outs = []

    def emit(f, q, value):
        O[f, q] = value
        outs.append(pltpu.make_async_copy(O.at[f, q], tile_of(oel, oac, f, q), sem.at[f * NQ + q]))
        outs[-1].start()

    for q in range(NQ):
        emit(7, q, tile_of(bel, bac, 7, q)[...])
    for t in range(24):
        c, part = t // 3, t % 3
        if part == 1:
            pa, pb = DB[2 * c], DB[2 * c + 1]
            top = jnp.where(left64, pa, pltpu.roll(pb, 64, 1))
            bot = jnp.where(left64, pltpu.roll(pa, 64, 1), pb)
            dx = jnp.concatenate([top, bot], axis=0)
        else:
            dx = DA[2 * c + part // 2]
        f, q = t // 4, t % 4
        for g in FED[f]:
            emit(g, q, tile_of(bel, bac, g, q)[...] + CO[g, q] * dx)
    for c in outs:
        c.wait()


def kernel(
    cnt, el, ac, em, am, cm, fc, dc, dw, elp, acp, wt,
    oel, oac, CO, DA, DB,
    F, H, XF, XP, XB, E, YA, YB, W, CM, C128, FC, PAIR, CNT, MEL, MAC,
    RC, RW, VS, VR, S, TH, TL, OH, ACC, SC, MK, HP, HN,
    s_load, s_med, s_small, s_fa, r_fa, s_fb, r_fb, s_ra, r_ra, s_rb, r_rb,
    s_rc, r_rc, s_rw, r_rw, s_v, r_v, s_h, r_h,
):
    me = lax.axis_index("line")
    zc = me // 2
    core = me % 2
    pt = lax.axis_index("patch")
    ly = lax.axis_index("layer")

    def line_of(dz, k):
        return ((zc + dz + 8) % 8) * 2 + k

    barrier = pltpu.get_barrier_semaphore()
    partners = [{"line": (me + o) % 16} for o in range(1, 16)]
    partners += [{"patch": (pt + o) % 4} for o in range(1, 4)]
    partners += [{"layer": (ly + o) % 4} for o in (1, 3)]
    for p in partners:
        pl.semaphore_signal(barrier, inc=1, device_id=p, device_id_type=MESH_ID)

    loads = {}
    for f in range(NF):
        for q in range(NQ):
            src = el.at[0, EL_OF[f], :, pl.ds(q * LANES, LANES)] if f in EL_OF else ac.at[0, AC_OF[f], :, pl.ds(q * LANES, LANES)]
            loads[f, q] = pltpu.make_async_copy(src, F.at[f, q], s_load.at[f * NQ + q])
            loads[f, q].start()
    small = [
        pltpu.make_async_copy(wt, W, s_small.at[0]),
        pltpu.make_async_copy(cm, CM, s_small.at[1]),
        pltpu.make_async_copy(fc.at[0, 0, 0], FC, s_small.at[2]),
        pltpu.make_async_copy(elp, PAIR.at[0], s_small.at[3]),
        pltpu.make_async_copy(acp, PAIR.at[1], s_small.at[4]),
        pltpu.make_async_copy(cnt, CNT, s_small.at[5]),
    ]
    for c in small:
        c.start()
    media = []
    for f in range(3):
        for q in range(NQ):
            media.append(pltpu.make_async_copy(em.at[0, f, :, pl.ds(q * LANES, LANES)], MEL.at[f, q], s_med.at[f * NQ + q]))
    for f in range(2):
        for q in range(NQ):
            media.append(pltpu.make_async_copy(am.at[0, f, :, pl.ds(q * LANES, LANES)], MAC.at[f, q], s_med.at[12 + f * NQ + q]))

    for f in range(6):
        for q in range(NQ):
            loads[f, q].wait()
    for f in range(6, 8):
        for q in range(NQ):
            loads[f, q].wait()

    pl.semaphore_wait(barrier, len(partners))

    reqs = []
    for o in range(1, 4):
        q = (pt + o) % 4
        reqs.append(pltpu.make_async_remote_copy(
            src_ref=dc.at[0, 0, 0, q], dst_ref=RC.at[o - 1], send_sem=s_rc.at[o - 1], recv_sem=r_rc.at[o - 1],
            device_id={"patch": q}, device_id_type=MESH_ID))
        reqs.append(pltpu.make_async_remote_copy(
            src_ref=dw.at[0, 0, 0, q], dst_ref=RW.at[o - 1], send_sem=s_rw.at[o - 1], recv_sem=r_rw.at[o - 1],
            device_id={"patch": q}, device_id_type=MESH_ID))
    for r in reqs:
        r.start()
    halo_up = pltpu.make_async_remote_copy(
        src_ref=F.at[:, 0], dst_ref=HN, send_sem=s_h.at[0], recv_sem=r_h.at[0],
        device_id={"layer": (ly + 3) % 4}, device_id_type=MESH_ID)
    halo_down = pltpu.make_async_remote_copy(
        src_ref=F.at[:, 3], dst_ref=HP, send_sem=s_h.at[1], recv_sem=r_h.at[1],
        device_id={"layer": (ly + 1) % 4}, device_id_type=MESH_ID)
    halo_up.start()
    halo_down.start()

    order = [(dz, k) for dz in (4, 3, -3, 2, -2, 1, -1) for k in (0, 1)]
    n_out = len(order)
    other = 1 - core

    def targets():
        for i, (dz, k) in enumerate(order):
            yield i, (zc + dz + 8) % 8, k
        yield n_out, zc, other

    def exchange(src_of, dst, send, recv):
        copies = []
        for i, c, k in targets():
            copies.append(pltpu.make_async_remote_copy(
                src_ref=src_of(c, k), dst_ref=dst.at[me], send_sem=send.at[i], recv_sem=recv.at[me],
                device_id={"line": c * 2 + k}, device_id_type=MESH_ID))
        own = pltpu.make_async_copy(src_of(zc, core), dst.at[me], recv.at[me])
        for r in copies:
            r.start()
        own.start()
        return copies

    def full_tile(c, k):
        t = 3 * c + 2 * k
        return F.at[t // 4, t % 4]

    fwd_a = exchange(full_tile, XF, s_fa, r_fa)
    left64 = lanes_of((32, LANES)) < 64
    for c in range(8):
        t = 3 * c + 1
        top = F[t // 4, t % 4, 0:32]
        bot = F[t // 4, t % 4, 32:64]
        H[2 * c] = jnp.where(left64, top, pltpu.roll(bot, 64, 1))
        H[2 * c + 1] = jnp.where(left64, pltpu.roll(top, 64, 1), bot)
    for m in media:
        m.start()

    def wait_recv(dst, recv, s):
        pltpu.make_async_copy(dst.at[s], dst.at[s], recv.at[s]).wait()

    for f in range(NF):
        for q in range(NQ):
            hi, lo = halves(F[f, q])
            TH[q * SL:(q + 1) * SL, f * LANES:(f + 1) * LANES] = hi
            TL[q * SL:(q + 1) * SL, f * LANES:(f + 1) * LANES] = lo
    fwd_b = exchange(lambda c, k: H.at[c * 2 + k], XP, s_fb, r_fb)
    for c in small:
        c.wait()
    S[...] = jnp.zeros_like(S)
    S[0:2 * MATCH] = jnp.concatenate([CM[...], CM[...]], axis=1)
    C128[...] = jnp.transpose(S[...])[0:LANES]
    E[...] = jnp.zeros_like(E)
    S[...] = jnp.zeros_like(S)
    lane_r = lanes_of((256, 256))
    lane_l = lanes_of((256, LANES))
    lane8 = lanes_of((256, LANES))

    def gather(i, carry):
        reqs_c = pltpu.make_async_copy(RC.at[i], RC.at[i], r_rc.at[i])
        reqs_w = pltpu.make_async_copy(RW.at[i], RW.at[i], r_rw.at[i])
        reqs_c.wait()
        reqs_w.wait()
        cells = RC[i]
        S[0:4] = (((cells >> 7) & 3) * SL + (cells >> 9)).astype(F32)
        S[4:8] = (cells & 127).astype(F32)
        S[8:12] = RW[i]
        cols = jnp.transpose(S[...])
        icols = cols.astype(jnp.int32)
        for s in range(4):
            hot = lane_r == icols[:, s:s + 1]
            OH[s * 256:(s + 1) * 256] = jnp.where(hot, 1.0, 0.0).astype(BF16)
        masks = [jnp.where(lane_l == icols[:, 4 + s:5 + s], cols[:, 8 + s:9 + s], 0.0) for s in range(4)]
        for s in range(4):
            ACC[s] = masks[s]
        v = jnp.zeros((256, LANES), F32)
        for fp in range(4):
            th = TH[:, fp * 256:(fp + 1) * 256]
            tl = TL[:, fp * 256:(fp + 1) * 256]
            total = None
            for s in range(4):
                hot = OH[s * 256:(s + 1) * 256]
                g = dot(hot, th) + dot(hot, tl)
                w = ACC[s]
                g = g * jnp.concatenate([w, w], axis=1)
                total = g if total is None else total + g
            for h in range(2):
                one = jnp.sum(total[:, h * LANES:(h + 1) * LANES], axis=1, keepdims=True)
                v = jnp.where(lane8 == fp * 2 + h, one, v)
        VS[i] = jnp.transpose(v)[0:8]
        return carry

    def response(i):
        q = (pt + 3 - i) % 4
        return pltpu.make_async_remote_copy(
            src_ref=VS.at[i], dst_ref=VR.at[i], send_sem=s_v.at[i], recv_sem=r_v.at[i],
            device_id={"patch": q}, device_id_type=MESH_ID)

    lax.fori_loop(0, 3, gather, 0)
    for i in range(3):
        response(i).start()

    def far_first(step):
        return ((8 - step) // 2) * (2 * (step % 2) - 1)

    arrivals = [(zc, core), (zc, other)] + [((zc + dz + 8) % 8, k) for dz in (1, -1, 2, -2, 3, -3, 4) for k in (0, 1)]

    def send_block(step, src, dst, send, recv):
        c = (zc + far_first(step) + 8) % 8
        for k in range(2):
            pltpu.make_async_remote_copy(
                src_ref=src.at[2 * c + k], dst_ref=dst.at[me], send_sem=send.at[2 * step + k], recv_sem=recv.at[me],
                device_id={"line": 2 * c + k}, device_id_type=MESH_ID).start()

    def send_last(src, dst, send, recv):
        pltpu.make_async_remote_copy(
            src_ref=src.at[2 * zc + other], dst_ref=dst.at[me], send_sem=send.at[14], recv_sem=recv.at[me],
            device_id={"line": 2 * zc + other}, device_id_type=MESH_ID).start()
        pltpu.make_async_copy(src.at[me], dst.at[me], recv.at[me]).start()

    def wait_sent(src, dst, send, recv):
        for i in range(15):
            pltpu.make_async_remote_copy(
                src_ref=src.at[0], dst_ref=dst.at[0], send_sem=send.at[i], recv_sem=recv.at[0],
                device_id={"line": 2 * zc + other}, device_id_type=MESH_ID).wait_send()

    def store_a(at, x):
        hi, lo = halves(x)
        XB[pl.ds(at, x.shape[0]), 0:LANES] = hi
        XB[pl.ds(at, x.shape[0]), LANES:] = lo

    for c, k in arrivals:
        s = 2 * c + k
        wait_recv(XF, r_fa, s)
        store_a(pl.multiple_of(s * SL, SL), XF[s])
    E[0:MATCH] = XF[15, SL - MATCH:]
    E[MATCH:2 * MATCH] = XF[0, 0:MATCH]
    store_a(1024, exact_dot(C128[...], E[...]))

    def rows_a(step, carry):
        i = (zc + far_first(step) + 8) % 8
        start = pl.multiple_of((7 - i) * LANES, LANES)
        wh = W[0, :, pl.ds(start, P_SIZE)]
        wl = W[1, :, pl.ds(start, P_SIZE)]
        y = dot(wh, XB[...])
        r = y[:, :LANES] + y[:, LANES:] + dot(wl, XB[:, 0:LANES])
        YA[2 * i] = r[0:SL]
        YA[2 * i + 1] = r[SL:]

        @pl.when(step > 0)
        def _():
            send_block(step - 1, YA, DA, s_ra, r_ra)

        return carry

    lax.fori_loop(0, 8, rows_a, 0)
    send_last(YA, DA, s_ra, r_ra)

    for i in range(3):
        wait_recv(VR, r_v, i)
    S[...] = jnp.zeros_like(S)
    row_r = rows_of((256, 256))
    slot = rows_of((256, LANES))
    for i in range(3):
        q = (pt + i + 1) % 4
        cells = FC[pl.ds(q, 1)]
        S[0:8] = VR[i]
        S[8:9] = (cells & 127).astype(F32)
        cols = jnp.transpose(S[...])
        target = ((cells >> 7) & 3) * SL + (cells >> 9)
        hot = jnp.where(row_r == target, 1.0, 0.0).astype(BF16)
        live = (lane_l == cols[:, 8:9].astype(jnp.int32)) & (slot < CNT[0, 0, 0, q])
        livef = jnp.where(live, 1.0, 0.0)
        part = dot(hot, livef.astype(BF16))
        MK[...] = part if i == 0 else MK[...] + part
        for fp in range(4):
            b = jnp.concatenate([livef * cols[:, 2 * fp:2 * fp + 1], livef * cols[:, 2 * fp + 1:2 * fp + 2]], axis=1)
            hi, lo = halves(b)
            part = dot(hot, hi) + dot(hot, lo)
            SC[fp] = part if i == 0 else SC[fp] + part

    def spread(x):
        r = pltpu.roll(x, 64, 1)
        return jnp.where(left64, x, r), jnp.where(left64, r, x)

    def store_b(at, x):
        hi, lo = halves(x)
        keep = lanes_of(x.shape) < 64
        XB[pl.ds(at, x.shape[0]), 0:LANES] = jnp.where(keep, hi.astype(F32), lo.astype(F32)).astype(BF16)

    for c, k in arrivals:
        s = 2 * c + k
        wait_recv(XP, r_fb, s)
        a, b = spread(XP[s])
        store_b(pl.multiple_of(s * SL, SL), a)
        store_b(pl.multiple_of(s * SL + 32, 32), b)
    E[0:MATCH] = spread(XP[15])[1][32 - MATCH:]
    E[MATCH:2 * MATCH] = spread(XP[0])[0][0:MATCH]
    store_b(1024, exact_dot(C128[...], E[...]))

    def rows_b(step, carry):
        i = (zc + far_first(step) + 8) % 8
        start = pl.multiple_of((7 - i) * LANES, LANES)
        x = XB[:, 0:LANES]
        y = dot(W[0, :, pl.ds(start, P_SIZE)], x) + dot(W[1, :, pl.ds(start, P_SIZE)], x)
        r = y + pltpu.roll(y, 64, 1)
        YB[2 * i] = jnp.where(left64, r[0:32], r[32:64])
        YB[2 * i + 1] = jnp.where(left64, r[64:96], r[96:128])

        @pl.when(step > 0)
        def _():
            send_block(step - 1, YB, DB, s_rb, r_rb)

        return carry

    lax.fori_loop(0, 8, rows_b, 0)
    send_last(YB, DB, s_rb, r_rb)

    pltpu.make_async_copy(HN, HN, r_h.at[0]).wait()
    pltpu.make_async_copy(HP, HP, r_h.at[1]).wait()
    for m in media:
        m.wait()
    lane = lanes_of((SL, LANES))
    first = ly == 0
    last = ly == 3
    S[...] = jnp.zeros_like(S)
    S[0:1, 0:64] = PAIR[0].astype(F32)
    S[1:2, 0:64] = PAIR[1].astype(F32)
    pair_cols = jnp.transpose(S[:, 0:LANES]).astype(jnp.int32)
    lane64 = lanes_of((SL, SL))
    pick_el = jnp.where(lane64 == pair_cols[0:64, 0:1], 1.0, 0.0)
    pick_ac = jnp.where(lane64 == pair_cols[0:64, 1:2], 1.0, 0.0)
    pressure = pltpu.roll(exact_dot(pick_el, HP[4]), 1, 1)
    velocity = pltpu.roll(exact_dot(pick_ac, HN[1]), LANES - 1, 1)
    zero_first = jnp.where(first, 0.0, 1.0)
    zero_last = jnp.where(last, 0.0, 1.0)
    one_first = jnp.where(first, 1.0, 0.0)
    one_last = jnp.where(last, 1.0, 0.0)

    for q in range(NQ):
        def dz(f):
            cur = F[f, q]
            prev = F[f, q - 1] if q else HP[f] * zero_first
            nxt = F[f, q + 1] if q < 3 else HN[f] * zero_last
            below = jnp.where(lane == LANES - 1, pltpu.roll(nxt, LANES - 1, 1), pltpu.roll(cur, LANES - 1, 1))
            above = jnp.where(lane == 0, pltpu.roll(prev, 1, 1), pltpu.roll(cur, 1, 1))
            return (below - above) * 0.125

        buoy, lam, mu = MEL[0, q], MEL[1, q], MEL[2, q]
        stiff = lam + 2.0 * mu
        bulk, obuoy = MAC[0, q], MAC[1, q]
        mask = MK[q * SL:(q + 1) * SL] > 0.5

        def put(f, base, coef):
            scat = SC[f // 2, q * SL:(q + 1) * SL, (f % 2) * LANES:(f % 2 + 1) * LANES]
            tile_of(oel, oac, f, q)[...] = jnp.where(mask, scat, base)
            if coef is not None:
                CO[f, q] = jnp.where(mask, 0.0, 0.25 * coef)

        dvz = dz(1)
        put(0, F[0, q] + buoy * dz(3), buoy)
        put(1, F[1, q] + buoy * dz(6), buoy)
        put(2, F[2, q] + lam * dvz, stiff)
        szz = F[6, q] + stiff * dvz
        if q == 0:
            szz = szz + jnp.where(lane == 0, one_first * 0.5 * (-pressure - F[6, q]), 0.0)
        put(6, szz, lam)
        put(3, F[3, q] + mu * dz(0), mu)
        put(4, F[4, q] - bulk * dz(7), -bulk)
        put(5, F[5, q], -obuoy)
        ovz = F[7, q] - obuoy * dz(4)
        if q == 3:
            ovz = ovz + jnp.where(lane == LANES - 1, one_last * 0.5 * (velocity - F[7, q]), 0.0)
        put(7, ovz, None)

    for i in range(16):
        wait_recv(DA, r_ra, i)
    for i in range(16):
        wait_recv(DB, r_rb, i)

    for r in reqs:
        r.wait_send()
    for i in range(3):
        response(i).wait_send()
    halo_up.wait_send()
    halo_down.wait_send()
    for group in (fwd_a, fwd_b):
        for r in group:
            r.wait_send()
    wait_sent(YA, DA, s_ra, r_ra)
    wait_sent(YB, DB, s_rb, r_rb)


def per_device(elastic, acoustic, el_media, ac_media, cont_matrix, fringe_cells, donor_cells, donor_weights, donor_counts, el_pair, ac_pair):
    anywhere = pl.BlockSpec(memory_space=pl.ANY)
    vm = pltpu.VMEM
    dma = pltpu.SemaphoreType.DMA
    scratch = [
        vm((NF, NQ, SL, LANES), F32),
        vm((16, 32, LANES), F32),
        vm((16, SL, LANES), F32),
        vm((16, 32, LANES), F32),
        vm((P_SIZE, 256), BF16),
        vm((LANES, LANES), F32),
        vm((16, SL, LANES), F32),
        vm((16, 32, LANES), F32),
        vm((2, 128, 2048), BF16),
        vm((2 * MATCH, 128), F32),
        vm((LANES, LANES), F32),
        vm((4, 256), jnp.int32),
        vm((2, 1, 64), jnp.int32),
        pltpu.SMEM((1, 1, 1, 4), jnp.int32),
        vm((3, NQ, SL, LANES), F32),
        vm((2, NQ, SL, LANES), F32),
        vm((3, 4, 256), jnp.int32),
        vm((3, 4, 256), F32),
        vm((3, 8, 256), F32),
        vm((3, 8, 256), F32),
        vm((LANES, 256), F32),
        vm((256, 1024), BF16),
        vm((256, 1024), BF16),
        vm((1024, 256), BF16),
        vm((4, 256, LANES), F32),
        vm((4, 256, 256), F32),
        vm((256, LANES), F32),
        vm((NF, SL, LANES), F32),
        vm((NF, SL, LANES), F32),
        dma((32,)), dma((20,)), dma((6,)),
        dma((15,)), dma((16,)), dma((15,)), dma((16,)),
        dma((15,)), dma((16,)), dma((15,)), dma((16,)),
        dma((3,)), dma((3,)), dma((3,)), dma((3,)), dma((3,)), dma((3,)),
        dma((2,)), dma((2,)),
    ]
    call = pl.pallas_call(
        kernel,
        out_shape=(
            vm(elastic.shape, F32), vm(acoustic.shape, F32), vm((7, NQ, SL, LANES), F32),
            vm((16, SL, LANES), F32), vm((16, 32, LANES), F32),
        ),
        in_specs=[anywhere] * 12,
        out_specs=(pl.BlockSpec(memory_space=pltpu.VMEM),) * 5,
        scratch_shapes=scratch,
        compiler_params=pltpu.CompilerParams(collective_id=0, has_side_effects=True),
    )
    parts = call(
        donor_counts, elastic, acoustic, el_media, ac_media, cont_matrix.T,
        fringe_cells, donor_cells, donor_weights, el_pair, ac_pair, jnp.asarray(derivative_rows()),
    )
    return pl.pallas_call(
        finish,
        out_shape=(jax.ShapeDtypeStruct(elastic.shape, F32), jax.ShapeDtypeStruct(acoustic.shape, F32)),
        in_specs=[pl.BlockSpec(memory_space=pltpu.VMEM)] * 5,
        out_specs=(anywhere, anywhere),
        scratch_shapes=[vm((NF, NQ, SL, LANES), F32), dma((32,))],
        compiler_params=pltpu.CompilerParams(vmem_limit_bytes=16 * 2**20),
    )(*parts)


def solution(mesh):
    fields = P("patch", None, "line", "layer")
    placed = (
        fields, fields, fields, fields,
        P(),
        P("patch", "line", "layer", None, None),
        P("patch", "line", "layer", None, None, None),
        P("patch", "line", "layer", None, None, None),
        P("patch", "line", "layer", None),
        P("patch", "line"),
        P("patch", "line"),
    )
    return jax.shard_map(per_device, mesh=mesh, in_specs=placed, out_specs=(fields, fields), check_vma=False)
```

```python
import functools
import math

import jax
import jax.numpy as jnp
import numpy as np
from jax import lax
from jax.experimental import pallas as pl
from jax.experimental.pallas import tpu as pltpu
from jax.sharding import PartitionSpec as P

P_SIZE = 1152
MATCH = 10
NF = 8
NQ = 4
SL = 64
LANES = 128
MESH_ID = pl.DeviceIdType.MESH
F32 = jnp.float32
BF16 = jnp.bfloat16

EL_OF = {0: 0, 1: 1, 2: 2, 3: 4, 6: 3}
AC_OF = {4: 0, 5: 1, 7: 2}
FED = {0: (2, 6), 1: (3,), 2: (0,), 3: (1,), 4: (5,), 5: (4,)}


def derivative_rows():
    d = np.arange(128)[:, None] - (np.arange(2048)[None, :] - 896)
    d = d % P_SIZE
    angle = np.where(d == 0, 1.0, np.pi * d / P_SIZE)
    value = np.where(d == 0, 0.0, (np.pi / P_SIZE) * np.where(d % 2 == 0, 1.0, -1.0) / np.tan(angle))
    high = value.astype(np.float32).astype(jnp.bfloat16)
    low = (value - high.astype(np.float64)).astype(np.float32).astype(jnp.bfloat16)
    return np.stack([high, low])


def halves(x):
    high = x.astype(BF16)
    low = (x - high.astype(F32)).astype(BF16)
    return high, low


def dot(a, b):
    return jnp.dot(a, b, preferred_element_type=F32)


def exact_dot(a, b):
    return jnp.dot(a, b, preferred_element_type=F32, precision=lax.Precision.HIGHEST)


def lanes_of(shape):
    return lax.broadcasted_iota(jnp.int32, shape, len(shape) - 1)


def rows_of(shape):
    return lax.broadcasted_iota(jnp.int32, shape, len(shape) - 2)


def tile_of(oel, oac, f, q):
    cols = pl.ds(q * LANES, LANES)
    return oel.at[0, EL_OF[f], :, cols] if f in EL_OF else oac.at[0, AC_OF[f], :, cols]


def finish(bel, bac, CO, DA, DB, oel, oac, O, sem):
    left64 = lanes_of((32, LANES)) < 64
    outs = []

    def emit(f, q, value):
        O[f, q] = value
        outs.append(pltpu.make_async_copy(O.at[f, q], tile_of(oel, oac, f, q), sem.at[f * NQ + q]))
        outs[-1].start()

    for q in range(NQ):
        emit(7, q, tile_of(bel, bac, 7, q)[...])
    for t in range(24):
        c, part = t // 3, t % 3
        if part == 1:
            pa, pb = DB[2 * c], DB[2 * c + 1]
            top = jnp.where(left64, pa, pltpu.roll(pb, 64, 1))
            bot = jnp.where(left64, pltpu.roll(pa, 64, 1), pb)
            dx = jnp.concatenate([top, bot], axis=0)
        else:
            dx = DA[2 * c + part // 2]
        f, q = t // 4, t % 4
        for g in FED[f]:
            emit(g, q, tile_of(bel, bac, g, q)[...] + CO[g, q] * dx)
    for c in outs:
        c.wait()


def kernel(
    cnt, el, ac, em, am, cm, fc, dc, dw, elp, acp, wt,
    oel, oac, CO, DA, DB,
    F, H, XF, XP, XB, E, YA, YB, W, CM, C128, FC, PAIR, CNT, MEL, MAC,
    RC, RW, VS, VR, S, TH, TL, OH, ACC, SC, MK, HP, HN,
    s_load, s_med, s_small, s_fa, r_fa, s_fb, r_fb, s_ra, r_ra, s_rb, r_rb,
    s_rc, r_rc, s_rw, r_rw, s_v, r_v, s_h, r_h,
):
    me = lax.axis_index("line")
    zc = me // 2
    core = me % 2
    pt = lax.axis_index("patch")
    ly = lax.axis_index("layer")

    def line_of(dz, k):
        return ((zc + dz + 8) % 8) * 2 + k

    barrier = pltpu.get_barrier_semaphore()
    partners = [{"line": (me + o) % 16} for o in range(1, 16)]
    partners += [{"patch": (pt + o) % 4} for o in range(1, 4)]
    partners += [{"layer": (ly + o) % 4} for o in (1, 3)]
    for p in partners:
        pl.semaphore_signal(barrier, inc=1, device_id=p, device_id_type=MESH_ID)

    loads = {}
    for f in range(NF):
        for q in range(NQ):
            src = el.at[0, EL_OF[f], :, pl.ds(q * LANES, LANES)] if f in EL_OF else ac.at[0, AC_OF[f], :, pl.ds(q * LANES, LANES)]
            loads[f, q] = pltpu.make_async_copy(src, F.at[f, q], s_load.at[f * NQ + q])
            loads[f, q].start()
    small = [
        pltpu.make_async_copy(wt, W, s_small.at[0]),
        pltpu.make_async_copy(cm, CM, s_small.at[1]),
        pltpu.make_async_copy(fc.at[0, 0, 0], FC, s_small.at[2]),
        pltpu.make_async_copy(elp, PAIR.at[0], s_small.at[3]),
        pltpu.make_async_copy(acp, PAIR.at[1], s_small.at[4]),
        pltpu.make_async_copy(cnt, CNT, s_small.at[5]),
    ]
    for c in small:
        c.start()
    media = []
    for f in range(3):
        for q in range(NQ):
            media.append(pltpu.make_async_copy(em.at[0, f, :, pl.ds(q * LANES, LANES)], MEL.at[f, q], s_med.at[f * NQ + q]))
    for f in range(2):
        for q in range(NQ):
            media.append(pltpu.make_async_copy(am.at[0, f, :, pl.ds(q * LANES, LANES)], MAC.at[f, q], s_med.at[12 + f * NQ + q]))

    for f in range(6):
        for q in range(NQ):
            loads[f, q].wait()
    left64 = lanes_of((32, LANES)) < 64
    for c in range(8):
        t = 3 * c + 1
        top = F[t // 4, t % 4, 0:32]
        bot = F[t // 4, t % 4, 32:64]
        H[2 * c] = jnp.where(left64, top, pltpu.roll(bot, 64, 1))
        H[2 * c + 1] = jnp.where(left64, pltpu.roll(top, 64, 1), bot)
    for f in range(6, 8):
        for q in range(NQ):
            loads[f, q].wait()

    pl.semaphore_wait(barrier, len(partners))

    reqs = []
    for o in range(1, 4):
        q = (pt + o) % 4
        reqs.append(pltpu.make_async_remote_copy(
            src_ref=dc.at[0, 0, 0, q], dst_ref=RC.at[o - 1], send_sem=s_rc.at[o - 1], recv_sem=r_rc.at[o - 1],
            device_id={"patch": q}, device_id_type=MESH_ID))
        reqs.append(pltpu.make_async_remote_copy(
            src_ref=dw.at[0, 0, 0, q], dst_ref=RW.at[o - 1], send_sem=s_rw.at[o - 1], recv_sem=r_rw.at[o - 1],
            device_id={"patch": q}, device_id_type=MESH_ID))
    for r in reqs:
        r.start()
    halo_up = pltpu.make_async_remote_copy(
        src_ref=F.at[:, 0], dst_ref=HN, send_sem=s_h.at[0], recv_sem=r_h.at[0],
        device_id={"layer": (ly + 3) % 4}, device_id_type=MESH_ID)
    halo_down = pltpu.make_async_remote_copy(
        src_ref=F.at[:, 3], dst_ref=HP, send_sem=s_h.at[1], recv_sem=r_h.at[1],
        device_id={"layer": (ly + 1) % 4}, device_id_type=MESH_ID)
    halo_up.start()
    halo_down.start()

    order = [(dz, k) for dz in (4, 3, -3, 2, -2, 1, -1) for k in (0, 1)]
    n_out = len(order)
    other = 1 - core

    def targets():
        for i, (dz, k) in enumerate(order):
            yield i, (zc + dz + 8) % 8, k
        yield n_out, zc, other

    def exchange(src_of, dst, send, recv):
        copies = []
        for i, c, k in targets():
            copies.append(pltpu.make_async_remote_copy(
                src_ref=src_of(c, k), dst_ref=dst.at[me], send_sem=send.at[i], recv_sem=recv.at[me],
                device_id={"line": c * 2 + k}, device_id_type=MESH_ID))
        own = pltpu.make_async_copy(src_of(zc, core), dst.at[me], recv.at[me])
        for r in copies:
            r.start()
        own.start()
        return copies

    def full_tile(c, k):
        t = 3 * c + 2 * k
        return F.at[t // 4, t % 4]

    fwd_b = exchange(lambda c, k: H.at[c * 2 + k], XP, s_fb, r_fb)
    fwd_a = exchange(full_tile, XF, s_fa, r_fa)
    for m in media:
        m.start()

    def wait_recv(dst, recv, s):
        pltpu.make_async_copy(dst.at[s], dst.at[s], recv.at[s]).wait()

    for f in range(NF):
        for q in range(NQ):
            hi, lo = halves(F[f, q])
            TH[q * SL:(q + 1) * SL, f * LANES:(f + 1) * LANES] = hi
            TL[q * SL:(q + 1) * SL, f * LANES:(f + 1) * LANES] = lo
    for c in small:
        c.wait()
    S[...] = jnp.zeros_like(S)
    S[0:2 * MATCH] = jnp.concatenate([CM[...], CM[...]], axis=1)
    C128[...] = jnp.transpose(S[...])[0:LANES]
    E[...] = jnp.zeros_like(E)
    S[...] = jnp.zeros_like(S)
    lane_r = lanes_of((256, 256))
    lane_l = lanes_of((256, LANES))
    lane8 = lanes_of((256, LANES))

    def gather(i, carry):
        reqs_c = pltpu.make_async_copy(RC.at[i], RC.at[i], r_rc.at[i])
        reqs_w = pltpu.make_async_copy(RW.at[i], RW.at[i], r_rw.at[i])
        reqs_c.wait()
        reqs_w.wait()
        cells = RC[i]
        S[0:4] = (((cells >> 7) & 3) * SL + (cells >> 9)).astype(F32)
        S[4:8] = (cells & 127).astype(F32)
        S[8:12] = RW[i]
        cols = jnp.transpose(S[...])
        icols = cols.astype(jnp.int32)
        for s in range(4):
            hot = lane_r == icols[:, s:s + 1]
            OH[s * 256:(s + 1) * 256] = jnp.where(hot, 1.0, 0.0).astype(BF16)
        masks = [jnp.where(lane_l == icols[:, 4 + s:5 + s], cols[:, 8 + s:9 + s], 0.0) for s in range(4)]
        for s in range(4):
            ACC[s] = masks[s]
        v = jnp.zeros((256, LANES), F32)
        for fp in range(4):
            th = TH[:, fp * 256:(fp + 1) * 256]
            tl = TL[:, fp * 256:(fp + 1) * 256]
            total = None
            for s in range(4):
                hot = OH[s * 256:(s + 1) * 256]
                g = dot(hot, th) + dot(hot, tl)
                w = ACC[s]
                g = g * jnp.concatenate([w, w], axis=1)
                total = g if total is None else total + g
            for h in range(2):
                one = jnp.sum(total[:, h * LANES:(h + 1) * LANES], axis=1, keepdims=True)
                v = jnp.where(lane8 == fp * 2 + h, one, v)
        VS[i] = jnp.transpose(v)[0:8]
        return carry

    def response(i):
        q = (pt + 3 - i) % 4
        return pltpu.make_async_remote_copy(
            src_ref=VS.at[i], dst_ref=VR.at[i], send_sem=s_v.at[i], recv_sem=r_v.at[i],
            device_id={"patch": q}, device_id_type=MESH_ID)

    lax.fori_loop(0, 3, gather, 0)
    for i in range(3):
        response(i).start()

    arrivals = [(zc, core), (zc, other)] + [((zc + dz + 8) % 8, k) for dz in (1, -1, 2, -2, 3, -3, 4) for k in (0, 1)]

    def send_block(i, src, dst, send, recv):
        for k in range(2):
            t = 2 * i + k

            @pl.when(t != me)
            def _():
                pltpu.make_async_remote_copy(
                    src_ref=src.at[t], dst_ref=dst.at[me], send_sem=send.at[t], recv_sem=recv.at[me],
                    device_id={"line": t}, device_id_type=MESH_ID).start()

            @pl.when(t == me)
            def _():
                pltpu.make_async_copy(src.at[me], dst.at[me], recv.at[me]).start()

    def wait_sent(src, dst, send, recv):
        for t in range(16):
            @pl.when(t != me)
            def _():
                pltpu.make_async_remote_copy(
                    src_ref=src.at[t], dst_ref=dst.at[me], send_sem=send.at[t], recv_sem=recv.at[me],
                    device_id={"line": t}, device_id_type=MESH_ID).wait_send()

    def store_a(at, x):
        hi, lo = halves(x)
        XB[pl.ds(at, x.shape[0]), 0:LANES] = hi
        XB[pl.ds(at, x.shape[0]), LANES:] = lo

    def spread(x):
        r = pltpu.roll(x, 64, 1)
        return jnp.where(left64, x, r), jnp.where(left64, r, x)

    def store_b(at, x):
        hi, lo = halves(x)
        keep = lanes_of(x.shape) < 64
        XB[pl.ds(at, x.shape[0]), 0:LANES] = jnp.where(keep, hi.astype(F32), lo.astype(F32)).astype(BF16)

    for c, k in arrivals:
        s = 2 * c + k
        wait_recv(XP, r_fb, s)
        a, b = spread(XP[s])
        store_b(pl.multiple_of(s * SL, SL), a)
        store_b(pl.multiple_of(s * SL + 32, 32), b)
    E[0:MATCH] = spread(XP[15])[1][32 - MATCH:]
    E[MATCH:2 * MATCH] = spread(XP[0])[0][0:MATCH]
    store_b(1024, exact_dot(C128[...], E[...]))

    def rows_b(i, carry):
        start = pl.multiple_of((7 - i) * LANES, LANES)
        x = XB[:, 0:LANES]
        y = dot(W[0, :, pl.ds(start, P_SIZE)], x) + dot(W[1, :, pl.ds(start, P_SIZE)], x)
        r = y + pltpu.roll(y, 64, 1)
        YB[2 * i] = jnp.where(left64, r[0:32], r[32:64])
        YB[2 * i + 1] = jnp.where(left64, r[64:96], r[96:128])

        @pl.when(i > 0)
        def _():
            send_block(i - 1, YB, DB, s_rb, r_rb)

        return carry

    lax.fori_loop(0, 8, rows_b, 0)
    send_block(7, YB, DB, s_rb, r_rb)

    for i in range(3):
        wait_recv(VR, r_v, i)
    S[...] = jnp.zeros_like(S)
    row_r = rows_of((256, 256))
    slot = rows_of((256, LANES))
    for i in range(3):
        q = (pt + i + 1) % 4
        cells = FC[pl.ds(q, 1)]
        S[0:8] = VR[i]
        S[8:9] = (cells & 127).astype(F32)
        cols = jnp.transpose(S[...])
        target = ((cells >> 7) & 3) * SL + (cells >> 9)
        hot = jnp.where(row_r == target, 1.0, 0.0).astype(BF16)
        live = (lane_l == cols[:, 8:9].astype(jnp.int32)) & (slot < CNT[0, 0, 0, q])
        livef = jnp.where(live, 1.0, 0.0)
        part = dot(hot, livef.astype(BF16))
        MK[...] = part if i == 0 else MK[...] + part
        for fp in range(4):
            b = jnp.concatenate([livef * cols[:, 2 * fp:2 * fp + 1], livef * cols[:, 2 * fp + 1:2 * fp + 2]], axis=1)
            hi, lo = halves(b)
            part = dot(hot, hi) + dot(hot, lo)
            SC[fp] = part if i == 0 else SC[fp] + part

    for c, k in arrivals:
        s = 2 * c + k
        wait_recv(XF, r_fa, s)
        store_a(pl.multiple_of(s * SL, SL), XF[s])
    E[0:MATCH] = XF[15, SL - MATCH:]
    E[MATCH:2 * MATCH] = XF[0, 0:MATCH]
    store_a(1024, exact_dot(C128[...], E[...]))

    def rows_a(i, carry):
        start = pl.multiple_of((7 - i) * LANES, LANES)
        wh = W[0, :, pl.ds(start, P_SIZE)]
        wl = W[1, :, pl.ds(start, P_SIZE)]
        y = dot(wh, XB[...])
        r = y[:, :LANES] + y[:, LANES:] + dot(wl, XB[:, 0:LANES])
        YA[2 * i] = r[0:SL]
        YA[2 * i + 1] = r[SL:]

        @pl.when(i > 0)
        def _():
            send_block(i - 1, YA, DA, s_ra, r_ra)

        return carry

    lax.fori_loop(0, 8, rows_a, 0)
    send_block(7, YA, DA, s_ra, r_ra)

    pltpu.make_async_copy(HN, HN, r_h.at[0]).wait()
    pltpu.make_async_copy(HP, HP, r_h.at[1]).wait()
    for m in media:
        m.wait()
    lane = lanes_of((SL, LANES))
    first = ly == 0
    last = ly == 3
    S[...] = jnp.zeros_like(S)
    S[0:1, 0:64] = PAIR[0].astype(F32)
    S[1:2, 0:64] = PAIR[1].astype(F32)
    pair_cols = jnp.transpose(S[:, 0:LANES]).astype(jnp.int32)
    lane64 = lanes_of((SL, SL))
    pick_el = jnp.where(lane64 == pair_cols[0:64, 0:1], 1.0, 0.0)
    pick_ac = jnp.where(lane64 == pair_cols[0:64, 1:2], 1.0, 0.0)
    pressure = pltpu.roll(exact_dot(pick_el, HP[4]), 1, 1)
    velocity = pltpu.roll(exact_dot(pick_ac, HN[1]), LANES - 1, 1)
    zero_first = jnp.where(first, 0.0, 1.0)
    zero_last = jnp.where(last, 0.0, 1.0)
    one_first = jnp.where(first, 1.0, 0.0)
    one_last = jnp.where(last, 1.0, 0.0)

    for q in range(NQ):
        def dz(f):
            cur = F[f, q]
            prev = F[f, q - 1] if q else HP[f] * zero_first
            nxt = F[f, q + 1] if q < 3 else HN[f] * zero_last
            below = jnp.where(lane == LANES - 1, pltpu.roll(nxt, LANES - 1, 1), pltpu.roll(cur, LANES - 1, 1))
            above = jnp.where(lane == 0, pltpu.roll(prev, 1, 1), pltpu.roll(cur, 1, 1))
            return (below - above) * 0.125

        buoy, lam, mu = MEL[0, q], MEL[1, q], MEL[2, q]
        stiff = lam + 2.0 * mu
        bulk, obuoy = MAC[0, q], MAC[1, q]
        mask = MK[q * SL:(q + 1) * SL] > 0.5

        def put(f, base, coef):
            scat = SC[f // 2, q * SL:(q + 1) * SL, (f % 2) * LANES:(f % 2 + 1) * LANES]
            tile_of(oel, oac, f, q)[...] = jnp.where(mask, scat, base)
            if coef is not None:
                CO[f, q] = jnp.where(mask, 0.0, 0.25 * coef)

        dvz = dz(1)
        put(0, F[0, q] + buoy * dz(3), buoy)
        put(1, F[1, q] + buoy * dz(6), buoy)
        put(2, F[2, q] + lam * dvz, stiff)
        szz = F[6, q] + stiff * dvz
        if q == 0:
            szz = szz + jnp.where(lane == 0, one_first * 0.5 * (-pressure - F[6, q]), 0.0)
        put(6, szz, lam)
        put(3, F[3, q] + mu * dz(0), mu)
        put(4, F[4, q] - bulk * dz(7), -bulk)
        put(5, F[5, q], -obuoy)
        ovz = F[7, q] - obuoy * dz(4)
        if q == 3:
            ovz = ovz + jnp.where(lane == LANES - 1, one_last * 0.5 * (velocity - F[7, q]), 0.0)
        put(7, ovz, None)

    for i in range(16):
        wait_recv(DA, r_ra, i)
    for i in range(16):
        wait_recv(DB, r_rb, i)

    for r in reqs:
        r.wait_send()
    for i in range(3):
        response(i).wait_send()
    halo_up.wait_send()
    halo_down.wait_send()
    for group in (fwd_a, fwd_b):
        for r in group:
            r.wait_send()
    wait_sent(YA, DA, s_ra, r_ra)
    wait_sent(YB, DB, s_rb, r_rb)


def per_device(elastic, acoustic, el_media, ac_media, cont_matrix, fringe_cells, donor_cells, donor_weights, donor_counts, el_pair, ac_pair):
    anywhere = pl.BlockSpec(memory_space=pl.ANY)
    vm = pltpu.VMEM
    dma = pltpu.SemaphoreType.DMA
    scratch = [
        vm((NF, NQ, SL, LANES), F32),
        vm((16, 32, LANES), F32),
        vm((16, SL, LANES), F32),
        vm((16, 32, LANES), F32),
        vm((P_SIZE, 256), BF16),
        vm((LANES, LANES), F32),
        vm((16, SL, LANES), F32),
        vm((16, 32, LANES), F32),
        vm((2, 128, 2048), BF16),
        vm((2 * MATCH, 128), F32),
        vm((LANES, LANES), F32),
        vm((4, 256), jnp.int32),
        vm((2, 1, 64), jnp.int32),
        pltpu.SMEM((1, 1, 1, 4), jnp.int32),
        vm((3, NQ, SL, LANES), F32),
        vm((2, NQ, SL, LANES), F32),
        vm((3, 4, 256), jnp.int32),
        vm((3, 4, 256), F32),
        vm((3, 8, 256), F32),
        vm((3, 8, 256), F32),
        vm((LANES, 256), F32),
        vm((256, 1024), BF16),
        vm((256, 1024), BF16),
        vm((1024, 256), BF16),
        vm((4, 256, LANES), F32),
        vm((4, 256, 256), F32),
        vm((256, LANES), F32),
        vm((NF, SL, LANES), F32),
        vm((NF, SL, LANES), F32),
        dma((32,)), dma((20,)), dma((6,)),
        dma((15,)), dma((16,)), dma((15,)), dma((16,)),
        dma((16,)), dma((16,)), dma((16,)), dma((16,)),
        dma((3,)), dma((3,)), dma((3,)), dma((3,)), dma((3,)), dma((3,)),
        dma((2,)), dma((2,)),
    ]
    call = pl.pallas_call(
        kernel,
        out_shape=(
            vm(elastic.shape, F32), vm(acoustic.shape, F32), vm((7, NQ, SL, LANES), F32),
            vm((16, SL, LANES), F32), vm((16, 32, LANES), F32),
        ),
        in_specs=[anywhere] * 12,
        out_specs=(pl.BlockSpec(memory_space=pltpu.VMEM),) * 5,
        scratch_shapes=scratch,
        compiler_params=pltpu.CompilerParams(collective_id=0, has_side_effects=True),
    )
    parts = call(
        donor_counts, elastic, acoustic, el_media, ac_media, cont_matrix.T,
        fringe_cells, donor_cells, donor_weights, el_pair, ac_pair, jnp.asarray(derivative_rows()),
    )
    return pl.pallas_call(
        finish,
        out_shape=(jax.ShapeDtypeStruct(elastic.shape, F32), jax.ShapeDtypeStruct(acoustic.shape, F32)),
        in_specs=[pl.BlockSpec(memory_space=pltpu.VMEM)] * 5,
        out_specs=(anywhere, anywhere),
        scratch_shapes=[vm((NF, NQ, SL, LANES), F32), dma((32,))],
        compiler_params=pltpu.CompilerParams(vmem_limit_bytes=16 * 2**20),
    )(*parts)


def solution(mesh):
    fields = P("patch", None, "line", "layer")
    placed = (
        fields, fields, fields, fields,
        P(),
        P("patch", "line", "layer", None, None),
        P("patch", "line", "layer", None, None, None),
        P("patch", "line", "layer", None, None, None),
        P("patch", "line", "layer", None),
        P("patch", "line"),
        P("patch", "line"),
    )
    return jax.shard_map(per_device, mesh=mesh, in_specs=placed, out_specs=(fields, fields), check_vma=False)
```

```python
import functools
import math

import jax
import jax.numpy as jnp
import numpy as np
from jax import lax
from jax.experimental import pallas as pl
from jax.experimental.pallas import tpu as pltpu
from jax.sharding import PartitionSpec as P

P_SIZE = 1152
MATCH = 10
NF = 8
NQ = 4
SL = 64
LANES = 128
MESH_ID = pl.DeviceIdType.MESH
F32 = jnp.float32
BF16 = jnp.bfloat16

EL_OF = {0: 0, 1: 1, 2: 2, 3: 4, 6: 3}
AC_OF = {4: 0, 5: 1, 7: 2}
FED = {0: (2, 6), 1: (3,), 2: (0,), 3: (1,), 4: (5,), 5: (4,)}


def derivative_rows():
    d = np.arange(128)[:, None] - (np.arange(2048)[None, :] - 896)
    d = d % P_SIZE
    angle = np.where(d == 0, 1.0, np.pi * d / P_SIZE)
    value = np.where(d == 0, 0.0, (np.pi / P_SIZE) * np.where(d % 2 == 0, 1.0, -1.0) / np.tan(angle))
    high = value.astype(np.float32).astype(jnp.bfloat16)
    low = (value - high.astype(np.float64)).astype(np.float32).astype(jnp.bfloat16)
    return np.stack([high, low])


def halves(x):
    high = x.astype(BF16)
    low = (x - high.astype(F32)).astype(BF16)
    return high, low


def dot(a, b):
    return jnp.dot(a, b, preferred_element_type=F32)


def exact_dot(a, b):
    return jnp.dot(a, b, preferred_element_type=F32, precision=lax.Precision.HIGHEST)


def lanes_of(shape):
    return lax.broadcasted_iota(jnp.int32, shape, len(shape) - 1)


def rows_of(shape):
    return lax.broadcasted_iota(jnp.int32, shape, len(shape) - 2)


def tile_of(oel, oac, f, q):
    cols = pl.ds(q * LANES, LANES)
    return oel.at[0, EL_OF[f], :, cols] if f in EL_OF else oac.at[0, AC_OF[f], :, cols]


def finish(bel, bac, CO, DA, DB, oel, oac, O, sem):
    left64 = lanes_of((32, LANES)) < 64
    outs = []

    def emit(f, q, value):
        O[f, q] = value
        outs.append(pltpu.make_async_copy(O.at[f, q], tile_of(oel, oac, f, q), sem.at[f * NQ + q]))
        outs[-1].start()

    for q in range(NQ):
        emit(7, q, tile_of(bel, bac, 7, q)[...])
    for t in range(24):
        c, part = t // 3, t % 3
        if part == 1:
            pa, pb = DB[2 * c], DB[2 * c + 1]
            top = jnp.where(left64, pa, pltpu.roll(pb, 64, 1))
            bot = jnp.where(left64, pltpu.roll(pa, 64, 1), pb)
            dx = jnp.concatenate([top, bot], axis=0)
        else:
            dx = DA[2 * c + part // 2]
        f, q = t // 4, t % 4
        for g in FED[f]:
            emit(g, q, tile_of(bel, bac, g, q)[...] + CO[g, q] * dx)
    for c in outs:
        c.wait()


def kernel(
    cnt, el, ac, em, am, cm, fc, dc, dw, elp, acp, wt,
    oel, oac, CO, DA, DB,
    F, H, XF, XP, XB, E, YA, YB, W, CM, C128, FC, PAIR, CNT, MEL, MAC,
    RC, RW, VS, VR, S, TH, TL, OH, ACC, SC, MK, HP, HN,
    s_load, s_med, s_small, s_fa, r_fa, s_fb, r_fb, s_ra, r_ra, s_rb, r_rb,
    s_rc, r_rc, s_rw, r_rw, s_v, r_v, s_h, r_h,
):
    me = lax.axis_index("line")
    zc = me // 2
    core = me % 2
    pt = lax.axis_index("patch")
    ly = lax.axis_index("layer")

    def line_of(dz, k):
        return ((zc + dz + 8) % 8) * 2 + k

    barrier = pltpu.get_barrier_semaphore()
    partners = [{"line": (me + o) % 16} for o in range(1, 16)]
    partners += [{"patch": (pt + o) % 4} for o in range(1, 4)]
    partners += [{"layer": (ly + o) % 4} for o in (1, 3)]
    for p in partners:
        pl.semaphore_signal(barrier, inc=1, device_id=p, device_id_type=MESH_ID)

    loads = {}
    for f in range(NF):
        for q in range(NQ):
            src = el.at[0, EL_OF[f], :, pl.ds(q * LANES, LANES)] if f in EL_OF else ac.at[0, AC_OF[f], :, pl.ds(q * LANES, LANES)]
            loads[f, q] = pltpu.make_async_copy(src, F.at[f, q], s_load.at[f * NQ + q])
            loads[f, q].start()
    small = [
        pltpu.make_async_copy(wt, W, s_small.at[0]),
        pltpu.make_async_copy(cm, CM, s_small.at[1]),
        pltpu.make_async_copy(fc.at[0, 0, 0], FC, s_small.at[2]),
        pltpu.make_async_copy(elp, PAIR.at[0], s_small.at[3]),
        pltpu.make_async_copy(acp, PAIR.at[1], s_small.at[4]),
        pltpu.make_async_copy(cnt, CNT, s_small.at[5]),
    ]
    for c in small:
        c.start()
    media = []
    for f in range(3):
        for q in range(NQ):
            media.append(pltpu.make_async_copy(em.at[0, f, :, pl.ds(q * LANES, LANES)], MEL.at[f, q], s_med.at[f * NQ + q]))
    for f in range(2):
        for q in range(NQ):
            media.append(pltpu.make_async_copy(am.at[0, f, :, pl.ds(q * LANES, LANES)], MAC.at[f, q], s_med.at[12 + f * NQ + q]))

    for f in range(6):
        for q in range(NQ):
            loads[f, q].wait()
    left64 = lanes_of((32, LANES)) < 64
    for c in range(8):
        t = 3 * c + 1
        top = F[t // 4, t % 4, 0:32]
        bot = F[t // 4, t % 4, 32:64]
        H[2 * c] = jnp.where(left64, top, pltpu.roll(bot, 64, 1))
        H[2 * c + 1] = jnp.where(left64, pltpu.roll(top, 64, 1), bot)

    pl.semaphore_wait(barrier, len(partners))

    order = [(dz, k) for dz in (4, 3, -3, 2, -2, 1, -1) for k in (0, 1)]
    n_out = len(order)
    other = 1 - core

    def targets():
        for i, (dz, k) in enumerate(order):
            yield i, (zc + dz + 8) % 8, k
        yield n_out, zc, other

    def exchange(src_of, dst, send, recv):
        copies = []
        for i, c, k in targets():
            copies.append(pltpu.make_async_remote_copy(
                src_ref=src_of(c, k), dst_ref=dst.at[me], send_sem=send.at[i], recv_sem=recv.at[me],
                device_id={"line": c * 2 + k}, device_id_type=MESH_ID))
        own = pltpu.make_async_copy(src_of(zc, core), dst.at[me], recv.at[me])
        for r in copies:
            r.start()
        own.start()
        return copies

    def full_tile(c, k):
        t = 3 * c + 2 * k
        return F.at[t // 4, t % 4]

    fwd_b = exchange(lambda c, k: H.at[c * 2 + k], XP, s_fb, r_fb)
    fwd_a = exchange(full_tile, XF, s_fa, r_fa)

    for f in range(6, 8):
        for q in range(NQ):
            loads[f, q].wait()

    reqs = []
    for o in range(1, 4):
        q = (pt + o) % 4
        reqs.append(pltpu.make_async_remote_copy(
            src_ref=dc.at[0, 0, 0, q], dst_ref=RC.at[o - 1], send_sem=s_rc.at[o - 1], recv_sem=r_rc.at[o - 1],
            device_id={"patch": q}, device_id_type=MESH_ID))
        reqs.append(pltpu.make_async_remote_copy(
            src_ref=dw.at[0, 0, 0, q], dst_ref=RW.at[o - 1], send_sem=s_rw.at[o - 1], recv_sem=r_rw.at[o - 1],
            device_id={"patch": q}, device_id_type=MESH_ID))
    for r in reqs:
        r.start()
    halo_up = pltpu.make_async_remote_copy(
        src_ref=F.at[:, 0], dst_ref=HN, send_sem=s_h.at[0], recv_sem=r_h.at[0],
        device_id={"layer": (ly + 3) % 4}, device_id_type=MESH_ID)
    halo_down = pltpu.make_async_remote_copy(
        src_ref=F.at[:, 3], dst_ref=HP, send_sem=s_h.at[1], recv_sem=r_h.at[1],
        device_id={"layer": (ly + 1) % 4}, device_id_type=MESH_ID)
    halo_up.start()
    halo_down.start()

    for m in media:
        m.start()

    def wait_recv(dst, recv, s):
        pltpu.make_async_copy(dst.at[s], dst.at[s], recv.at[s]).wait()

    for f in range(NF):
        for q in range(NQ):
            hi, lo = halves(F[f, q])
            TH[q * SL:(q + 1) * SL, f * LANES:(f + 1) * LANES] = hi
            TL[q * SL:(q + 1) * SL, f * LANES:(f + 1) * LANES] = lo
    for c in small:
        c.wait()
    S[...] = jnp.zeros_like(S)
    S[0:2 * MATCH] = jnp.concatenate([CM[...], CM[...]], axis=1)
    C128[...] = jnp.transpose(S[...])[0:LANES]
    E[...] = jnp.zeros_like(E)
    S[...] = jnp.zeros_like(S)
    lane_r = lanes_of((256, 256))
    lane_l = lanes_of((256, LANES))
    lane8 = lanes_of((256, LANES))

    def gather(i, carry):
        reqs_c = pltpu.make_async_copy(RC.at[i], RC.at[i], r_rc.at[i])
        reqs_w = pltpu.make_async_copy(RW.at[i], RW.at[i], r_rw.at[i])
        reqs_c.wait()
        reqs_w.wait()
        cells = RC[i]
        S[0:4] = (((cells >> 7) & 3) * SL + (cells >> 9)).astype(F32)
        S[4:8] = (cells & 127).astype(F32)
        S[8:12] = RW[i]
        cols = jnp.transpose(S[...])
        icols = cols.astype(jnp.int32)
        for s in range(4):
            hot = lane_r == icols[:, s:s + 1]
            OH[s * 256:(s + 1) * 256] = jnp.where(hot, 1.0, 0.0).astype(BF16)
        masks = [jnp.where(lane_l == icols[:, 4 + s:5 + s], cols[:, 8 + s:9 + s], 0.0) for s in range(4)]
        for s in range(4):
            ACC[s] = masks[s]
        v = jnp.zeros((256, LANES), F32)
        for fp in range(4):
            th = TH[:, fp * 256:(fp + 1) * 256]
            tl = TL[:, fp * 256:(fp + 1) * 256]
            total = None
            for s in range(4):
                hot = OH[s * 256:(s + 1) * 256]
                g = dot(hot, th) + dot(hot, tl)
                w = ACC[s]
                g = g * jnp.concatenate([w, w], axis=1)
                total = g if total is None else total + g
            for h in range(2):
                one = jnp.sum(total[:, h * LANES:(h + 1) * LANES], axis=1, keepdims=True)
                v = jnp.where(lane8 == fp * 2 + h, one, v)
        VS[i] = jnp.transpose(v)[0:8]
        return carry

    def response(i):
        q = (pt + 3 - i) % 4
        return pltpu.make_async_remote_copy(
            src_ref=VS.at[i], dst_ref=VR.at[i], send_sem=s_v.at[i], recv_sem=r_v.at[i],
            device_id={"patch": q}, device_id_type=MESH_ID)

    lax.fori_loop(0, 3, gather, 0)
    for i in range(3):
        response(i).start()

    arrivals = [(zc, core), (zc, other)] + [((zc + dz + 8) % 8, k) for dz in (1, -1, 2, -2, 3, -3, 4) for k in (0, 1)]

    def send_block(i, src, dst, send, recv):
        for k in range(2):
            t = 2 * i + k

            @pl.when(t != me)
            def _():
                pltpu.make_async_remote_copy(
                    src_ref=src.at[t], dst_ref=dst.at[me], send_sem=send.at[t], recv_sem=recv.at[me],
                    device_id={"line": t}, device_id_type=MESH_ID).start()

            @pl.when(t == me)
            def _():
                pltpu.make_async_copy(src.at[me], dst.at[me], recv.at[me]).start()

    def wait_sent(src, dst, send, recv):
        for t in range(16):
            @pl.when(t != me)
            def _():
                pltpu.make_async_remote_copy(
                    src_ref=src.at[t], dst_ref=dst.at[me], send_sem=send.at[t], recv_sem=recv.at[me],
                    device_id={"line": t}, device_id_type=MESH_ID).wait_send()

    def store_a(at, x):
        hi, lo = halves(x)
        XB[pl.ds(at, x.shape[0]), 0:LANES] = hi
        XB[pl.ds(at, x.shape[0]), LANES:] = lo

    def spread(x):
        r = pltpu.roll(x, 64, 1)
        return jnp.where(left64, x, r), jnp.where(left64, r, x)

    def store_b(at, x):
        hi, lo = halves(x)
        keep = lanes_of(x.shape) < 64
        XB[pl.ds(at, x.shape[0]), 0:LANES] = jnp.where(keep, hi.astype(F32), lo.astype(F32)).astype(BF16)

    for c, k in arrivals:
        s = 2 * c + k
        wait_recv(XP, r_fb, s)
        a, b = spread(XP[s])
        store_b(pl.multiple_of(s * SL, SL), a)
        store_b(pl.multiple_of(s * SL + 32, 32), b)
    E[0:MATCH] = spread(XP[15])[1][32 - MATCH:]
    E[MATCH:2 * MATCH] = spread(XP[0])[0][0:MATCH]
    store_b(1024, exact_dot(C128[...], E[...]))

    def rows_b(i, carry):
        start = pl.multiple_of((7 - i) * LANES, LANES)
        x = XB[:, 0:LANES]
        y = dot(W[0, :, pl.ds(start, P_SIZE)], x) + dot(W[1, :, pl.ds(start, P_SIZE)], x)
        r = y + pltpu.roll(y, 64, 1)
        YB[2 * i] = jnp.where(left64, r[0:32], r[32:64])
        YB[2 * i + 1] = jnp.where(left64, r[64:96], r[96:128])

        @pl.when(i > 0)
        def _():
            send_block(i - 1, YB, DB, s_rb, r_rb)

        return carry

    lax.fori_loop(0, 8, rows_b, 0)
    send_block(7, YB, DB, s_rb, r_rb)

    for i in range(3):
        wait_recv(VR, r_v, i)
    S[...] = jnp.zeros_like(S)
    row_r = rows_of((256, 256))
    slot = rows_of((256, LANES))
    for i in range(3):
        q = (pt + i + 1) % 4
        cells = FC[pl.ds(q, 1)]
        S[0:8] = VR[i]
        S[8:9] = (cells & 127).astype(F32)
        cols = jnp.transpose(S[...])
        target = ((cells >> 7) & 3) * SL + (cells >> 9)
        hot = jnp.where(row_r == target, 1.0, 0.0).astype(BF16)
        live = (lane_l == cols[:, 8:9].astype(jnp.int32)) & (slot < CNT[0, 0, 0, q])
        livef = jnp.where(live, 1.0, 0.0)
        part = dot(hot, livef.astype(BF16))
        MK[...] = part if i == 0 else MK[...] + part
        for fp in range(4):
            b = jnp.concatenate([livef * cols[:, 2 * fp:2 * fp + 1], livef * cols[:, 2 * fp + 1:2 * fp + 2]], axis=1)
            hi, lo = halves(b)
            part = dot(hot, hi) + dot(hot, lo)
            SC[fp] = part if i == 0 else SC[fp] + part

    for c, k in arrivals:
        s = 2 * c + k
        wait_recv(XF, r_fa, s)
        store_a(pl.multiple_of(s * SL, SL), XF[s])
    E[0:MATCH] = XF[15, SL - MATCH:]
    E[MATCH:2 * MATCH] = XF[0, 0:MATCH]
    store_a(1024, exact_dot(C128[...], E[...]))

    def rows_a(i, carry):
        start = pl.multiple_of((7 - i) * LANES, LANES)
        wh = W[0, :, pl.ds(start, P_SIZE)]
        wl = W[1, :, pl.ds(start, P_SIZE)]
        y = dot(wh, XB[...])
        r = y[:, :LANES] + y[:, LANES:] + dot(wl, XB[:, 0:LANES])
        YA[2 * i] = r[0:SL]
        YA[2 * i + 1] = r[SL:]

        @pl.when(i > 0)
        def _():
            send_block(i - 1, YA, DA, s_ra, r_ra)

        return carry

    lax.fori_loop(0, 8, rows_a, 0)
    send_block(7, YA, DA, s_ra, r_ra)

    pltpu.make_async_copy(HN, HN, r_h.at[0]).wait()
    pltpu.make_async_copy(HP, HP, r_h.at[1]).wait()
    for m in media:
        m.wait()
    lane = lanes_of((SL, LANES))
    first = ly == 0
    last = ly == 3
    S[...] = jnp.zeros_like(S)
    S[0:1, 0:64] = PAIR[0].astype(F32)
    S[1:2, 0:64] = PAIR[1].astype(F32)
    pair_cols = jnp.transpose(S[:, 0:LANES]).astype(jnp.int32)
    lane64 = lanes_of((SL, SL))
    pick_el = jnp.where(lane64 == pair_cols[0:64, 0:1], 1.0, 0.0)
    pick_ac = jnp.where(lane64 == pair_cols[0:64, 1:2], 1.0, 0.0)
    pressure = pltpu.roll(exact_dot(pick_el, HP[4]), 1, 1)
    velocity = pltpu.roll(exact_dot(pick_ac, HN[1]), LANES - 1, 1)
    zero_first = jnp.where(first, 0.0, 1.0)
    zero_last = jnp.where(last, 0.0, 1.0)
    one_first = jnp.where(first, 1.0, 0.0)
    one_last = jnp.where(last, 1.0, 0.0)

    for q in range(NQ):
        def dz(f):
            cur = F[f, q]
            prev = F[f, q - 1] if q else HP[f] * zero_first
            nxt = F[f, q + 1] if q < 3 else HN[f] * zero_last
            below = jnp.where(lane == LANES - 1, pltpu.roll(nxt, LANES - 1, 1), pltpu.roll(cur, LANES - 1, 1))
            above = jnp.where(lane == 0, pltpu.roll(prev, 1, 1), pltpu.roll(cur, 1, 1))
            return (below - above) * 0.125

        buoy, lam, mu = MEL[0, q], MEL[1, q], MEL[2, q]
        stiff = lam + 2.0 * mu
        bulk, obuoy = MAC[0, q], MAC[1, q]
        mask = MK[q * SL:(q + 1) * SL] > 0.5

        def put(f, base, coef):
            scat = SC[f // 2, q * SL:(q + 1) * SL, (f % 2) * LANES:(f % 2 + 1) * LANES]
            tile_of(oel, oac, f, q)[...] = jnp.where(mask, scat, base)
            if coef is not None:
                CO[f, q] = jnp.where(mask, 0.0, 0.25 * coef)

        dvz = dz(1)
        put(0, F[0, q] + buoy * dz(3), buoy)
        put(1, F[1, q] + buoy * dz(6), buoy)
        put(2, F[2, q] + lam * dvz, stiff)
        szz = F[6, q] + stiff * dvz
        if q == 0:
            szz = szz + jnp.where(lane == 0, one_first * 0.5 * (-pressure - F[6, q]), 0.0)
        put(6, szz, lam)
        put(3, F[3, q] + mu * dz(0), mu)
        put(4, F[4, q] - bulk * dz(7), -bulk)
        put(5, F[5, q], -obuoy)
        ovz = F[7, q] - obuoy * dz(4)
        if q == 3:
            ovz = ovz + jnp.where(lane == LANES - 1, one_last * 0.5 * (velocity - F[7, q]), 0.0)
        put(7, ovz, None)

    for i in range(16):
        wait_recv(DA, r_ra, i)
    for i in range(16):
        wait_recv(DB, r_rb, i)

    for r in reqs:
        r.wait_send()
    for i in range(3):
        response(i).wait_send()
    halo_up.wait_send()
    halo_down.wait_send()
    for group in (fwd_a, fwd_b):
        for r in group:
            r.wait_send()
    wait_sent(YA, DA, s_ra, r_ra)
    wait_sent(YB, DB, s_rb, r_rb)


def per_device(elastic, acoustic, el_media, ac_media, cont_matrix, fringe_cells, donor_cells, donor_weights, donor_counts, el_pair, ac_pair):
    anywhere = pl.BlockSpec(memory_space=pl.ANY)
    vm = pltpu.VMEM
    dma = pltpu.SemaphoreType.DMA
    scratch = [
        vm((NF, NQ, SL, LANES), F32),
        vm((16, 32, LANES), F32),
        vm((16, SL, LANES), F32),
        vm((16, 32, LANES), F32),
        vm((P_SIZE, 256), BF16),
        vm((LANES, LANES), F32),
        vm((16, SL, LANES), F32),
        vm((16, 32, LANES), F32),
        vm((2, 128, 2048), BF16),
        vm((2 * MATCH, 128), F32),
        vm((LANES, LANES), F32),
        vm((4, 256), jnp.int32),
        vm((2, 1, 64), jnp.int32),
        pltpu.SMEM((1, 1, 1, 4), jnp.int32),
        vm((3, NQ, SL, LANES), F32),
        vm((2, NQ, SL, LANES), F32),
        vm((3, 4, 256), jnp.int32),
        vm((3, 4, 256), F32),
        vm((3, 8, 256), F32),
        vm((3, 8, 256), F32),
        vm((LANES, 256), F32),
        vm((256, 1024), BF16),
        vm((256, 1024), BF16),
        vm((1024, 256), BF16),
        vm((4, 256, LANES), F32),
        vm((4, 256, 256), F32),
        vm((256, LANES), F32),
        vm((NF, SL, LANES), F32),
        vm((NF, SL, LANES), F32),
        dma((32,)), dma((20,)), dma((6,)),
        dma((15,)), dma((16,)), dma((15,)), dma((16,)),
        dma((16,)), dma((16,)), dma((16,)), dma((16,)),
        dma((3,)), dma((3,)), dma((3,)), dma((3,)), dma((3,)), dma((3,)),
        dma((2,)), dma((2,)),
    ]
    call = pl.pallas_call(
        kernel,
        out_shape=(
            vm(elastic.shape, F32), vm(acoustic.shape, F32), vm((7, NQ, SL, LANES), F32),
            vm((16, SL, LANES), F32), vm((16, 32, LANES), F32),
        ),
        in_specs=[anywhere] * 12,
        out_specs=(pl.BlockSpec(memory_space=pltpu.VMEM),) * 5,
        scratch_shapes=scratch,
        compiler_params=pltpu.CompilerParams(collective_id=0, has_side_effects=True),
    )
    parts = call(
        donor_counts, elastic, acoustic, el_media, ac_media, cont_matrix.T,
        fringe_cells, donor_cells, donor_weights, el_pair, ac_pair, jnp.asarray(derivative_rows()),
    )
    return pl.pallas_call(
        finish,
        out_shape=(jax.ShapeDtypeStruct(elastic.shape, F32), jax.ShapeDtypeStruct(acoustic.shape, F32)),
        in_specs=[pl.BlockSpec(memory_space=pltpu.VMEM)] * 5,
        out_specs=(anywhere, anywhere),
        scratch_shapes=[vm((NF, NQ, SL, LANES), F32), dma((32,))],
        compiler_params=pltpu.CompilerParams(vmem_limit_bytes=16 * 2**20),
    )(*parts)


def solution(mesh):
    fields = P("patch", None, "line", "layer")
    placed = (
        fields, fields, fields, fields,
        P(),
        P("patch", "line", "layer", None, None),
        P("patch", "line", "layer", None, None, None),
        P("patch", "line", "layer", None, None, None),
        P("patch", "line", "layer", None),
        P("patch", "line"),
        P("patch", "line"),
    )
    return jax.shard_map(per_device, mesh=mesh, in_specs=placed, out_specs=(fields, fields), check_vma=False)
```
